32 devices in a mesh: groups: 2 (over x), genome: 16 (over z, y, core).
Axes of the slice: x: 2, y: 2, z: 4, core: 2. Of those that a mesh axis runs over, the one named last changes fastest.
Arguments:
- factor: bfloat16 [96, 2048, 256], P(('groups', 'genome')), parts along dimension 0, may hold values from -0.5 to 0.5
- normals: bfloat16 [96, 256, 1024], P(('groups', 'genome')), parts along dimension 0, may hold values from -6 to 6
- block_len: int32 [96], P(('groups', 'genome')), parts along dimension 0, may hold values from 256 to 2048, as said below
- block_rank: int32 [96], P(('groups', 'genome')), parts along dimension 0, may hold values from 32 to 256, as said below
- gene_span: int32 [2048, 2], P(('groups', 'genome')), parts along dimension 0, may hold values from 0 to 98304, as said below
- gene_pathways: int32 [2048, 4], P('groups'), parts along dimension 0, may hold values from 0 to 4095, as said below
Outputs:
- pathway_score: float32 [8192, 1024], P(('groups', 'genome')), parts along dimension 0
The draws below stay inside these ranges and needn't reach their ends.
There are 2 independent parts, one for each index of `groups`. The reference program is written for one: setup_inputs(seed, part) draws one part's arguments, and reference() takes and returns one part's arrays. A program takes and returns all parts, laid end to end along the dimension named above; each array names one. Nothing has to cross between parts.
Inputs may be any that keep to these rules, and one draw needn't show every extreme that they name: `block_len`: some block of every draw holds all 2048 slots. `block_rank`: some block of every draw keeps all 256 columns. `gene_span`: genes of rows j * 64 to (j + 1) * 64 - 1 start at a valid slot within slots j * 6144 to (j + 1) * 6144 - 1 and end no later than (j + 1) * 6144 + 2048, never past 98304; the end exceeds the start; some gene of every draw ends exactly 2048 slots past the range of its start. Each gene names 4 different pathways, and every pathway is named by some gene. With q = g * 4 + m, the pathway gene_pathways[g, m] lies in rows r * 256 to (r + 1) * 256 - 1 with r = q % 16, so the genes of one index of genome name at most 16 pathways of one such range, and exactly 16 for some range.
All inputs are finite; a program needn't handle non-finite values.
Results may differ from the reference program's by a relative error of at most 0.0021.
Values may be sent and summed in bfloat16 or wider, within the bound.
No kernel may reach another device: no remote copies, remote signals or barrier semaphores. Data moves between devices by JAX's collectives and lax.ppermute only.
A program may use at most 128 MiB of HBM per device.

```python
import jax
import jax.numpy as jnp
from jax import lax

BLK_DEV = 3
BVAR = 2048
RANK = 256
SIMS = 1024
GENES_DEV = 64
PATHWAYS = 4096
MEMB = 4
BLOCKS = 48
VAR_DEV = 6144
VARIANTS = 98304
GENES = 1024
N_GENOME = 16


def make_layout(key):
    layout_key = jax.random.fold_in(key, 7)
    keys = jax.random.split(layout_key, 6)
    lengths = jax.random.randint(keys[0], (BLOCKS,), BVAR // 8, BVAR + 1)
    fullest = jax.random.randint(keys[1], (), 0, BLOCKS)
    lengths = jnp.where(jnp.arange(BLOCKS) == fullest, BVAR, lengths).astype(jnp.int32)
    device_count = BLOCKS // BLK_DEV
    shape = (device_count, GENES_DEV)
    device_ids = jnp.arange(device_count, dtype=jnp.int32)[:, None] + jnp.zeros(shape, jnp.int32)
    gene_ids = jnp.arange(GENES_DEV, dtype=jnp.int32)[None, :] + jnp.zeros(shape, jnp.int32)
    straddle = (gene_ids == GENES_DEV - 1) & (device_ids < device_count - 1)
    slots = jax.random.randint(keys[2], shape, 0, BLK_DEV)
    slots = jnp.where(straddle, BLK_DEV - 1, slots)
    block_ids = device_ids * BLK_DEV + slots
    block_sizes = jnp.take(lengths, block_ids)
    rows_in = jax.random.randint(keys[3], shape, 0, block_sizes)
    starts = block_ids * BVAR + rows_in
    widths = jax.random.randint(keys[4], shape, BVAR // 4, 2 * BVAR)
    device_end = (device_ids + 1) * VAR_DEV
    inner_end = jnp.minimum(starts + widths, device_end)
    reach = jax.random.randint(keys[5], shape, 1, BVAR + 1)
    reach = jnp.where(device_ids == 0, BVAR, reach)
    ends = jnp.where(straddle, device_end + reach, inner_end)
    spans = jnp.stack([starts, ends], axis=-1).reshape(device_count * GENES_DEV, 2).astype(jnp.int32)
    return (lengths, spans)


def draw_block_len(key, part):
    return make_layout(key)[0]


def draw_gene_span(key, part):
    return make_layout(key)[1]


def draw_block_rank(key, part):
    rank_key = jax.random.fold_in(key, 9)
    first_key, second_key = jax.random.split(rank_key)
    ranks = jax.random.randint(first_key, (BLOCKS,), RANK // 8, RANK + 1)
    fullest = jax.random.randint(second_key, (), 0, BLOCKS)
    return jnp.where(jnp.arange(BLOCKS) == fullest, RANK, ranks).astype(jnp.int32)


def draw_gene_pathways(key, part):
    member_key = jax.random.fold_in(key, 11)
    first_key, second_key = jax.random.split(member_key)
    device_count = GENES // GENES_DEV
    path_rows = PATHWAYS // device_count
    pairs = jnp.arange(GENES * MEMB, dtype=jnp.int32)
    owner = pairs % device_count
    order = pairs // device_count
    perms = jax.vmap(lambda single: jax.random.permutation(single, path_rows))(jax.random.split(first_key, device_count))
    extra = jax.random.randint(second_key, (GENES * MEMB,), 0, path_rows)
    picked = perms[owner, order % path_rows]
    local = jnp.where(order < path_rows, picked, extra)
    return (owner * path_rows + local).reshape(GENES, MEMB).astype(jnp.int32)


def level_of(own_key, dims, pieces, low, top_value):
    level = 1.0
    for axis_at, blocks in pieces:
        heights = jax.random.uniform(jax.random.fold_in(jax.random.fold_in(own_key, 6), axis_at), (blocks,), jnp.float32, low / len(pieces), top_value / len(pieces))
        level = level * jnp.repeat(jnp.exp(heights), dims[axis_at] // blocks).reshape((-1,) + (1,) * (len(dims) - 1 - axis_at))
    return level


def scatter_about(rng, shape, spread, bound, shards=(), kind=jnp.bfloat16):
    loudness = level_of(rng, shape, shards, -0.22, 0.18) if shards else 1.0
    drawn = jax.random.normal(rng, shape, jnp.float32) * spread * loudness
    return jnp.minimum(jnp.maximum(drawn, -bound), bound).astype(kind)


def setup_inputs(seed: int = 0, part: int = 0) -> dict:
    key_list = jax.random.split(jax.random.key(seed), 7)
    own_keys = jax.random.split(jax.random.fold_in(key_list[6], part), 7)
    factor = scatter_about(own_keys[0], (BLOCKS, BVAR, RANK), (RANK // 2) ** -0.5, 0.5, ((0, 16),))
    normals = scatter_about(own_keys[1], (BLOCKS, RANK, SIMS), 1.0, 6.0, ((0, 16),))
    block_len = draw_block_len(jax.random.fold_in(jax.random.fold_in(key_list[6], part), 71), part)
    block_rank = draw_block_rank(jax.random.fold_in(jax.random.fold_in(key_list[6], part), 71), part)
    gene_span = draw_gene_span(jax.random.fold_in(jax.random.fold_in(key_list[6], part), 71), part)
    gene_pathways = draw_gene_pathways(jax.random.fold_in(jax.random.fold_in(key_list[6], part), 71), part)
    return dict(factor=factor, normals=normals, block_len=block_len, block_rank=block_rank, gene_span=gene_span, gene_pathways=gene_pathways)


def covered(positions, spans):
    lower = spans[:, 0][:, None]
    upper = spans[:, 1][:, None]
    return ((positions[None, :] >= lower) & (positions[None, :] < upper)).astype(jnp.float32)


def reference(factor, normals, block_len, block_rank, gene_span, gene_pathways):
    def device_sums(index):
        chosen = jnp.minimum(index * BLK_DEV + jnp.arange(BLK_DEV + 1, dtype=jnp.int32), BLOCKS - 1).astype(jnp.int32)
        factors = jnp.take(factor, chosen, axis=0).astype(jnp.float32)
        vectors = jnp.take(normals, chosen, axis=0).astype(jnp.float32)
        ranks = jnp.take(block_rank, chosen, axis=0)
        lengths = jnp.take(block_len, chosen, axis=0)
        kept = jnp.arange(RANK, dtype=jnp.int32)[None, :, None] < ranks[:, None, None]
        vectors = jnp.where(kept, vectors, jnp.zeros_like(vectors))
        coloured = jnp.einsum("bvk,bks->bvs", factors, vectors, precision=lax.Precision.HIGHEST)
        positions = index * VAR_DEV + jnp.arange((BLK_DEV + 1) * BVAR, dtype=jnp.int32)
        usable = (jnp.arange(BVAR, dtype=jnp.int32)[None, :] < lengths[:, None]).reshape(-1)
        usable = usable & (positions < VARIANTS)
        squares = jnp.where(usable[:, None], (coloured * coloured).reshape((BLK_DEV + 1) * BVAR, SIMS), 0.0)
        spans = lax.dynamic_slice_in_dim(gene_span, (index * GENES_DEV).astype(jnp.int32), GENES_DEV, 0)
        return jnp.dot(covered(positions, spans), squares, precision=lax.Precision.HIGHEST)

    totals = lax.map(device_sums, jnp.arange(N_GENOME, dtype=jnp.int32)).reshape(GENES, SIMS)
    gene_stat = (totals / BVAR).astype(jnp.bfloat16)
    member = jnp.any(gene_pathways[:, :, None] == jnp.arange(PATHWAYS, dtype=jnp.int32)[None, None, :], axis=1)
    path_count = jnp.sum(member.astype(jnp.float32), axis=0)
    path_sum = jnp.dot(member.astype(jnp.bfloat16).T, gene_stat, preferred_element_type=jnp.float32)
    return path_sum / path_count[:, None]
```

```python
import functools

import jax
import jax.numpy as jnp
from jax import lax
from jax.experimental import pallas as pl
from jax.experimental.pallas import tpu as pltpu
from jax.sharding import PartitionSpec as P

PATHWAYS = 4096
QUAD = 4
CHUNK = 512
COLS = 256
VMEM = pltpu.MemorySpace.VMEM
SMEM = pltpu.MemorySpace.SMEM


def to_column(row, classes):
    genes = row.shape[1]
    each = genes // classes
    at = lax.broadcasted_iota(jnp.int32, (genes, genes), 0)
    lane = lax.broadcasted_iota(jnp.int32, (genes, genes), 1)
    hit = lane == (at % each) * classes + at // each
    values = jnp.where(hit, row.astype(jnp.float32), 0.0)
    return jnp.sum(values, axis=1, keepdims=True).astype(jnp.int32)


def block_kernel(classes, sets, info, *refs):
    spans, (factor, normals) = refs[:sets], refs[sets:sets + 2]
    outs = refs[sets + 2:2 * sets + 2]
    vectors, lower, upper = refs[2 * sets + 2:]
    genes = spans[0].shape[1]
    step = pl.program_id(0)
    base, length, rank = info[0], info[1], info[2]

    @pl.when(step == 0)
    def _():
        row = lax.broadcasted_iota(jnp.int32, normals.shape[1:], 0)
        vectors[...] = jnp.where(row < rank, normals[0].astype(jnp.float32), 0.0).astype(jnp.bfloat16)
        for at in range(sets):
            span = spans[at][...]
            rows = pl.ds(at * genes, genes)
            lower[rows, :] = to_column(span[0:1], classes) - base
            upper[rows, :] = jnp.minimum(to_column(span[1:2], classes) - base, length)
            outs[at][...] = jnp.zeros(outs[at].shape, jnp.float32)

    @pl.when(step * CHUNK < length)
    def _():
        slot = step * CHUNK + lax.broadcasted_iota(jnp.int32, (sets * genes, CHUNK), 1)
        mask = (slot >= lower[...]) & (slot < upper[...])
        mask = jnp.where(mask, 1.0, 0.0).astype(jnp.bfloat16)
        sims = vectors.shape[1]
        for col in range(0, sims, COLS):
            cols = slice(col, col + COLS)
            coloured = jnp.dot(factor[0], vectors[:, cols], preferred_element_type=jnp.float32)
            square = coloured * coloured
            high = square.astype(jnp.bfloat16)
            low = (square - high.astype(jnp.float32)).astype(jnp.bfloat16)
            total = jnp.dot(mask, high, preferred_element_type=jnp.float32)
            total = total + jnp.dot(mask, low, preferred_element_type=jnp.float32)
            for at in range(sets):
                outs[at][:, cols] += total[at * genes:(at + 1) * genes]


def block_sums(block, classes, info, spans, factor, normals):
    sets = len(spans)
    genes = spans[0].shape[1]
    _, capacity, rank_cap = factor.shape
    sims = normals.shape[2]
    whole = pl.BlockSpec((genes, sims), lambda i, info: (0, 0))
    last = lambda i, info: (block, jnp.minimum(i, (info[1] - 1) // CHUNK), 0)
    return pl.pallas_call(
        functools.partial(block_kernel, classes, sets),
        out_shape=[jax.ShapeDtypeStruct((genes, sims), jnp.float32)] * sets,
        grid_spec=pltpu.PrefetchScalarGridSpec(
            num_scalar_prefetch=1,
            grid=(capacity // CHUNK,),
            in_specs=[pl.BlockSpec((2, genes), lambda i, info: (0, 0))] * sets
            + [
                pl.BlockSpec((1, CHUNK, rank_cap), last),
                pl.BlockSpec((1, rank_cap, sims), lambda i, info: (block, 0, 0)),
            ],
            out_specs=[whole] * sets,
            scratch_shapes=[
                pltpu.VMEM((rank_cap, sims), jnp.bfloat16),
                pltpu.VMEM((sets * genes, 1), jnp.int32),
                pltpu.VMEM((sets * genes, 1), jnp.int32),
            ],
        ),
        cost_estimate=pl.CostEstimate(
            flops=6 * capacity * rank_cap * sims, bytes_accessed=4 << 20, transcendentals=0
        ),
        name=f"block{block}",
    )(info, *spans, factor, normals)


def combine_kernel(classes, capacity, where, first, second, third, back, *refs):
    outs, stat = refs[:-1], refs[-1]
    each = outs[0].shape[0]
    total = first[...] + second[...] + third[...] + back[...]
    total = total / capacity
    for at in range(classes):
        stat[at] = total[at * each:(at + 1) * each]
    for ahead in range(classes):
        outs[ahead][...] = stat[lax.rem(where[0] + ahead, classes)].astype(jnp.bfloat16)


def combine(classes, capacity, where, parts):
    genes, sims = parts[0].shape
    piece = jax.ShapeDtypeStruct((genes // classes, sims), jnp.bfloat16)
    return pl.pallas_call(
        functools.partial(combine_kernel, classes, capacity),
        out_shape=[piece] * classes,
        in_specs=[pl.BlockSpec(memory_space=SMEM)] + [pl.BlockSpec(memory_space=VMEM)] * 4,
        out_specs=[pl.BlockSpec(memory_space=VMEM)] * classes,
        scratch_shapes=[pltpu.VMEM((classes, genes // classes, sims), jnp.float32)],
        name="combine",
    )(where, *parts)


def member_kernel(classes, flips, genes_dev, where, paths, member, count):
    plane, inner = where[0], where[1]
    rows, pairs = member.shape
    genes = paths.shape[1]
    each = genes_dev // classes
    device = plane * QUAD + inner
    own = paths[pl.ds(inner, 1), :] - device * rows
    own = jnp.where((own >= 0) & (own < rows), own, 0).astype(jnp.float32)
    own = jnp.broadcast_to(own, (8, genes)).astype(jnp.bfloat16)
    col = lax.broadcasted_iota(jnp.int32, (genes, pairs), 1)
    gene = lax.broadcasted_iota(jnp.int32, (genes, pairs), 0)
    part = col // genes_dev
    source_in = jnp.zeros(col.shape, jnp.int32)
    for at, flip in enumerate(flips):
        source_in = jnp.where(part == at, inner ^ flip, source_in)
    behind = (col % genes_dev) // each
    source_plane = plane - behind
    source_plane = jnp.where(source_plane < 0, source_plane + classes, source_plane)
    source = source_plane * QUAD + source_in
    named = source * genes_dev + (col % each) * classes + plane
    pick = jnp.where(gene == named, 1.0, 0.0).astype(jnp.bfloat16)
    ids = jnp.dot(own, pick, preferred_element_type=jnp.float32)[0:1]
    row = lax.broadcasted_iota(jnp.int32, (rows, pairs), 0).astype(jnp.float32)
    found = jnp.where(row == ids, 1.0, 0.0)
    member[...] = found.astype(jnp.bfloat16)
    count[...] = jnp.sum(found, axis=1, keepdims=True)


def members(classes, flips, genes_dev, rows, where, paths):
    pairs = QUAD * genes_dev
    return pl.pallas_call(
        functools.partial(member_kernel, classes, flips, genes_dev),
        out_shape=[
            jax.ShapeDtypeStruct((rows, pairs), jnp.bfloat16),
            jax.ShapeDtypeStruct((rows, 1), jnp.float32),
        ],
        in_specs=[pl.BlockSpec(memory_space=SMEM), pl.BlockSpec(memory_space=VMEM)],
        out_specs=[pl.BlockSpec(memory_space=VMEM)] * 2,
        name="members",
    )(where, paths)


def score_kernel(member, count, first, second, third, fourth, out):
    genes = first.shape[0]
    total = jnp.zeros(out.shape, jnp.float32)
    for at, part in enumerate((first, second, third, fourth)):
        total = total + jnp.dot(
            member[:, at * genes:(at + 1) * genes], part[...], preferred_element_type=jnp.float32
        )
    out[...] = total / count[...]


def score(member, count, parts):
    rows = member.shape[0]
    return pl.pallas_call(
        score_kernel,
        out_shape=jax.ShapeDtypeStruct((rows, parts[0].shape[1]), jnp.float32),
        in_specs=[pl.BlockSpec(memory_space=VMEM)] * 6,
        out_specs=pl.BlockSpec(memory_space=VMEM),
        name="score",
    )(member, count, *parts)


def local(factor, normals, block_len, block_rank, gene_span, gene_pathways):
    block_count, capacity, _ = factor.shape
    genes = gene_span.shape[0]
    device = lax.axis_index("genome")
    size = lax.axis_size("genome")
    classes = size // QUAD
    each = genes // classes
    plane, inner = device // QUAD, device % QUAD
    send = functools.partial(lax.ppermute, axis_name="genome")

    own = gene_span.T
    before = send(own, perm=[(i, i + 1) for i in range(size - 1)])

    def info(block):
        base = (device * block_count + block) * capacity
        return jnp.stack([base, block_len[block], block_rank[block]])

    sums = functools.partial(block_sums, factor=factor, normals=normals)
    (first,) = sums(1, classes, info(1), [own])
    second, lent = sums(0, classes, info(0), [own, before])
    back = send(lent, perm=[(i + 1, i) for i in range(size - 1)])
    (third,) = sums(2, classes, info(2), [own])
    where = jnp.stack([plane, inner])
    pieces = combine(classes, float(capacity), where, [first, second, third, back])

    arrived = [pieces[0]]
    for ahead in range(1, classes):
        route = [
            (c * QUAD + j, (c + ahead) % classes * QUAD + j)
            for c in range(classes)
            for j in range(QUAD)
        ]
        arrived.append(send(pieces[ahead], perm=route))
    mine = jnp.concatenate(arrived, axis=0)
    flip = lambda x, bit: send(x, perm=[(i, i ^ bit) for i in range(size)])
    across = flip(mine, 2)
    partner = flip(mine, 1)
    corner = flip(across, 1)

    rows = PATHWAYS // size
    member, count = members(classes, (0, 2, 1, 3), genes, rows, where, gene_pathways.T)
    return score(member, count, [mine, across, partner, corner])


def solution(mesh):
    in_specs = (
        P(("groups", "genome"), None, None),
        P(("groups", "genome"), None, None),
        P(("groups", "genome")),
        P(("groups", "genome")),
        P(("groups", "genome"), None),
        P("groups", None),
    )
    out_specs = P(("groups", "genome"), None)
    return jax.shard_map(local, mesh=mesh, in_specs=in_specs, out_specs=out_specs, check_vma=False)
```

```python
import functools

import jax
import jax.numpy as jnp
from jax import lax
from jax.experimental import pallas as pl
from jax.experimental.pallas import tpu as pltpu
from jax.sharding import PartitionSpec as P

PATHWAYS = 4096
QUAD = 4
CHUNK = 512
COLS = 256
LANES = 128
VMEM = pltpu.MemorySpace.VMEM
SMEM = pltpu.MemorySpace.SMEM


def gene_sums(prefix, parts, spans, out, base, length, classes):
    genes = spans.shape[1]
    each = genes // classes
    tiles = prefix.shape[0]

    @pl.loop(0, genes // 8)
    def _(group):
        for slot in range(8):
            spot = group * 8 + slot
            gene = (spot % each) * classes + spot // each
            lower = jnp.clip(spans[0, gene] - base, 0, length)
            upper = jnp.clip(spans[1, gene] - base, 0, length)
            for tile in range(tiles):
                parts[tile, slot * 8:slot * 8 + 8, :] = (
                    prefix[tile, pl.ds(upper, 8), :] - prefix[tile, pl.ds(lower, 8), :]
                )
        place = pl.ds(pl.multiple_of(group * 8, 8), 8)
        for tile in range(tiles):
            total = parts[tile, pl.ds(0, 8, stride=8), :]
            for sub in range(1, 8):
                total = total + parts[tile, pl.ds(sub, 8, stride=8), :]
            out[place, tile * LANES:(tile + 1) * LANES] = total


def running_sums(factor, normals, rank, length, vectors, prefix):
    rank_cap, sims = normals.shape
    tiles = sims // LANES
    row = lax.broadcasted_iota(jnp.int32, (rank_cap, LANES), 0)
    keep = jnp.where(row < rank, 1.0, 0.0).astype(jnp.bfloat16)
    for tile in range(tiles):
        cols = slice(tile * LANES, (tile + 1) * LANES)
        vectors[:, cols] = normals[:, cols] * keep
        prefix[tile, 0:8, :] = jnp.zeros((8, LANES), jnp.float32)

    @pl.loop(0, (length() + CHUNK - 1) // CHUNK)
    def _(chunk):
        start = pl.multiple_of(chunk * CHUNK, CHUNK)
        rows = factor[pl.ds(start, CHUNK), :]
        for col in range(0, sims, COLS):
            coloured = jnp.dot(rows, vectors[:, col:col + COLS], preferred_element_type=jnp.float32)
            square = coloured * coloured
            for part in range(COLS // LANES):
                tile = col // LANES + part
                run = prefix[tile, pl.ds(start, 8), :]
                for at in range(0, CHUNK, 8):
                    run = run + square[at:at + 8, part * LANES:(part + 1) * LANES]
                    prefix[tile, pl.ds(start + at + 8, 8), :] = run


def opening_kernel(classes, lens, ranks, spans, factor, normals, out, next_factor, next_normals, table,
                   lens_in, ranks_in, spans_in, factor_in, normals_in, vectors, prefix, parts, sems):
    block_count, capacity, _ = factor.shape
    copies = [
        pltpu.make_async_copy(source, target, sems.at[at])
        for at, (source, target) in enumerate([
            (ranks, ranks_in), (lens, lens_in), (normals.at[1], normals_in), (factor.at[1], factor_in),
            (spans, spans_in), (normals.at[0], next_normals.at[0]), (factor.at[0], next_factor.at[0]),
            (normals.at[2], next_normals.at[1]), (factor.at[2], next_factor.at[1]),
        ])
    ]
    for copy in copies:
        copy.start()
    for copy in copies[:4]:
        copy.wait()
    for block in range(block_count):
        table[block:block + 1, :] = jnp.full((1, LANES), ranks_in[block], jnp.int32)
        table[block_count + block:block_count + block + 1, :] = jnp.full((1, LANES), lens_in[block], jnp.int32)
    running_sums(factor_in, normals_in, ranks_in[1], lambda: lens_in[1], vectors, prefix)
    copies[4].wait()
    base = (lax.axis_index("genome") * block_count + 1) * capacity
    gene_sums(prefix, parts, spans_in, out, base, lens_in[1], classes)
    for copy in copies[5:]:
        copy.wait()


def block_kernel(block, at, block_count, classes, sets, table, *refs):
    spans, (factor, normals) = refs[:sets], refs[sets:sets + 2]
    outs = refs[sets + 2:2 * sets + 2]
    table_in, spans_in, vectors, prefix, parts, sems = refs[2 * sets + 2:]
    capacity = factor.shape[1]
    copies = [pltpu.make_async_copy(table, table_in, sems.at[0])]
    for own in range(sets):
        copies.append(pltpu.make_async_copy(spans[own], spans_in.at[own], sems.at[1 + own]))
    for copy in copies:
        copy.start()
    factor, normals = factor.at[at], normals.at[at]

    def length():
        for copy in copies:
            copy.wait()
        return table_in[block_count + block, 0]

    running_sums(factor, normals, table[block:block + 1, :], length, vectors, prefix)
    base = (lax.axis_index("genome") * block_count + block) * capacity
    for own in range(sets):
        gene_sums(prefix, parts, spans_in.at[own], outs[own], base, table_in[block_count + block, 0], classes)


def work_space(capacity, rank_cap, sims):
    return [
        pltpu.VMEM((rank_cap, sims), jnp.bfloat16),
        pltpu.VMEM((sims // LANES, capacity + 8, LANES), jnp.float32),
        pltpu.VMEM((sims // LANES, 64, LANES), jnp.float32),
    ]


ANY, IN_VMEM = pl.BlockSpec(memory_space=pl.ANY), pl.BlockSpec(memory_space=VMEM)
IN_HBM = pl.BlockSpec(memory_space=pltpu.MemorySpace.HBM)


def opening(classes, lens, ranks, spans, factor, normals):
    genes = spans.shape[1]
    block_count, capacity, rank_cap = factor.shape
    sims = normals.shape[2]
    shape = jax.ShapeDtypeStruct
    return pl.pallas_call(
        functools.partial(opening_kernel, classes),
        out_shape=[
            shape((genes, sims), jnp.float32),
            shape((block_count - 1, capacity, rank_cap), factor.dtype),
            shape((block_count - 1, rank_cap, sims), normals.dtype),
            shape((8, LANES), jnp.int32),
        ],
        in_specs=[IN_HBM] * 5,
        out_specs=[IN_VMEM] * 4,
        scratch_shapes=[
            pltpu.SMEM((block_count,), jnp.int32),
            pltpu.SMEM((block_count,), jnp.int32),
            pltpu.SMEM((2, genes), jnp.int32),
            pltpu.VMEM((capacity, rank_cap), factor.dtype),
            pltpu.VMEM((rank_cap, sims), normals.dtype),
        ] + work_space(capacity, rank_cap, sims) + [pltpu.SemaphoreType.DMA((9,))],
        compiler_params=pltpu.CompilerParams(vmem_limit_bytes=24 << 20),
        name="opening",
    )(lens, ranks, spans, factor, normals)


def block_sums(block, at, block_count, classes, table, spans, factor, normals):
    sets = len(spans)
    genes = spans[0].shape[1]
    _, capacity, rank_cap = factor.shape
    sims = normals.shape[2]
    return pl.pallas_call(
        functools.partial(block_kernel, block, at, block_count, classes, sets),
        out_shape=[jax.ShapeDtypeStruct((genes, sims), jnp.float32)] * sets,
        in_specs=[IN_VMEM] + [ANY] * sets + [IN_VMEM] * 2,
        out_specs=[IN_VMEM] * sets,
        scratch_shapes=[pltpu.SMEM((8, LANES), jnp.int32), pltpu.SMEM((sets, 2, genes), jnp.int32)]
        + work_space(capacity, rank_cap, sims) + [pltpu.SemaphoreType.DMA((1 + sets,))],
        compiler_params=pltpu.CompilerParams(vmem_limit_bytes=20 << 20),
        cost_estimate=pl.CostEstimate(
            flops=6 * capacity * rank_cap * sims, bytes_accessed=4 << 20, transcendentals=0
        ),
        name=f"block{block}",
    )(table, *spans, factor, normals)


def combine_kernel(classes, capacity, first, second, third, back, *refs):
    outs, stat = refs[:-1], refs[-1]
    each = outs[0].shape[0]
    total = first[...] + second[...] + third[...] + back[...]
    total = total / capacity
    for at in range(classes):
        stat[at] = total[at * each:(at + 1) * each]
    plane = lax.axis_index("genome") // QUAD
    for ahead in range(classes):
        outs[ahead][...] = stat[lax.rem(plane + ahead, classes)].astype(jnp.bfloat16)


def combine(classes, capacity, parts):
    genes, sims = parts[0].shape
    piece = jax.ShapeDtypeStruct((genes // classes, sims), jnp.bfloat16)
    return pl.pallas_call(
        functools.partial(combine_kernel, classes, capacity),
        out_shape=[piece] * classes,
        in_specs=[pl.BlockSpec(memory_space=VMEM)] * 4,
        out_specs=[pl.BlockSpec(memory_space=VMEM)] * classes,
        scratch_shapes=[pltpu.VMEM((classes, genes // classes, sims), jnp.float32)],
        compiler_params=pltpu.CompilerParams(vmem_limit_bytes=8 << 20),
        name="combine",
    )(*parts)


def member_kernel(classes, flips, genes_dev, paths, member, share):
    device = lax.axis_index("genome")
    plane, inner = device // QUAD, device % QUAD
    rows, pairs = member.shape
    genes = paths.shape[1]
    each = genes_dev // classes
    own = paths[pl.ds(inner, 1), :] - device * rows
    own = jnp.where((own >= 0) & (own < rows), own, 0).astype(jnp.float32)
    own = jnp.broadcast_to(own, (8, genes)).astype(jnp.bfloat16)
    col = lax.broadcasted_iota(jnp.int32, (genes, pairs), 1)
    gene = lax.broadcasted_iota(jnp.int32, (genes, pairs), 0)
    part = col // genes_dev
    source_in = jnp.zeros(col.shape, jnp.int32)
    for at, flip in enumerate(flips):
        source_in = jnp.where(part == at, inner ^ flip, source_in)
    behind = (col % genes_dev) // each
    source_plane = plane - behind
    source_plane = jnp.where(source_plane < 0, source_plane + classes, source_plane)
    source = source_plane * QUAD + source_in
    named = source * genes_dev + (col % each) * classes + plane
    pick = jnp.where(gene == named, 1.0, 0.0).astype(jnp.bfloat16)
    ids = jnp.dot(own, pick, preferred_element_type=jnp.float32)[0:1]
    row = lax.broadcasted_iota(jnp.int32, (rows, pairs), 0).astype(jnp.float32)
    found = jnp.where(row == ids, 1.0, 0.0)
    member[...] = found.astype(jnp.bfloat16)
    share[...] = 1.0 / jnp.sum(found, axis=1, keepdims=True)


def members(classes, flips, genes_dev, rows, paths):
    pairs = QUAD * genes_dev
    return pl.pallas_call(
        functools.partial(member_kernel, classes, flips, genes_dev),
        out_shape=[
            jax.ShapeDtypeStruct((rows, pairs), jnp.bfloat16),
            jax.ShapeDtypeStruct((rows, 1), jnp.float32),
        ],
        in_specs=[pl.BlockSpec(memory_space=VMEM)],
        out_specs=[pl.BlockSpec(memory_space=VMEM)] * 2,
        compiler_params=pltpu.CompilerParams(vmem_limit_bytes=16 << 20),
        name="members",
    )(paths)


def score_kernel(member, share, *refs):
    parts, (out, made, sems) = refs[:-3], refs[-3:]
    copies = []
    for at in range(made.shape[0]):
        cols = slice(at * COLS, (at + 1) * COLS)
        genes = jnp.concatenate([part[:, cols] for part in parts], axis=0)
        made[at] = jnp.dot(member[...], genes, preferred_element_type=jnp.float32) * share[...]
        copies.append(pltpu.make_async_copy(made.at[at], out.at[:, cols], sems.at[at]))
        copies[-1].start()
    for copy in copies:
        copy.wait()


def score(member, share, parts):
    rows, pairs = member.shape
    _, sims = parts[0].shape
    return pl.pallas_call(
        score_kernel,
        out_shape=jax.ShapeDtypeStruct((rows, sims), jnp.float32),
        in_specs=[IN_VMEM] * (2 + len(parts)),
        out_specs=ANY,
        scratch_shapes=[
            pltpu.VMEM((sims // COLS, rows, COLS), jnp.float32),
            pltpu.SemaphoreType.DMA((sims // COLS,)),
        ],
        compiler_params=pltpu.CompilerParams(vmem_limit_bytes=16 << 20),
        name="score",
    )(member, share, *parts)


def local(factor, normals, block_len, block_rank, gene_span, gene_pathways):
    block_count, capacity, _ = factor.shape
    genes = gene_span.shape[0]
    size = lax.axis_size("genome")
    classes = size // QUAD
    send = functools.partial(lax.ppermute, axis_name="genome")

    own = gene_span.T
    held = lambda x: pltpu.with_memory_space_constraint(x, pltpu.MemorySpace.HBM)
    first, *ahead_of, table = opening(classes, *map(held, (block_len, block_rank, own, factor, normals)))
    own, first = lax.optimization_barrier((own, first))
    before = send(own, perm=[(i, i + 1) for i in range(size - 1)])
    rows = PATHWAYS // size
    member, share = members(classes, (0, 2, 1, 3), genes, rows, gene_pathways.T)
    before, member, share = lax.optimization_barrier((before, member, share))
    sums = lambda block, at, spans: block_sums(block, at, block_count, classes, table, spans, *ahead_of)
    second, lent = sums(0, 0, [own, before])
    back = send(lent, perm=[(i + 1, i) for i in range(size - 1)])
    (third,) = sums(2, 1, [own])
    pieces = combine(classes, float(capacity), [first, second, third, back])

    arrived = [pieces[0]]
    for ahead in range(1, classes):
        route = [
            (c * QUAD + j, (c + ahead) % classes * QUAD + j)
            for c in range(classes)
            for j in range(QUAD)
        ]
        arrived.append(send(pieces[ahead], perm=route))
    mine = jnp.concatenate(arrived, axis=0)
    flip = lambda x, bit: send(x, perm=[(i, i ^ bit) for i in range(size)])
    across = flip(mine, 2)
    partner = flip(mine, 1)
    corner = flip(across, 1)

    return score(member, share, [mine, across, partner, corner])


def solution(mesh):
    in_specs = (
        P(("groups", "genome"), None, None),
        P(("groups", "genome"), None, None),
        P(("groups", "genome")),
        P(("groups", "genome")),
        P(("groups", "genome"), None),
        P("groups", None),
    )
    out_specs = P(("groups", "genome"), None)
    return jax.shard_map(local, mesh=mesh, in_specs=in_specs, out_specs=out_specs, check_vma=False)
```

```python
import functools

import jax
import jax.numpy as jnp
from jax import lax
from jax.experimental import pallas as pl
from jax.experimental.pallas import tpu as pltpu
from jax.sharding import PartitionSpec as P

PATHWAYS = 4096
QUAD = 4
CHUNK = 1024
COLS = 256
LANES = 128
VMEM = pltpu.MemorySpace.VMEM
SMEM = pltpu.MemorySpace.SMEM


def reduce_parts(parts, side, out, first):
    for tile in range(parts.shape[1]):
        total = parts[side, tile, pl.ds(0, 8, stride=8), :]
        for sub in range(1, 8):
            total = total + parts[side, tile, pl.ds(sub, 8, stride=8), :]
        out[first:first + 8, tile * LANES:(tile + 1) * LANES] = total


def class_major(place, each, classes):
    return place % each * classes + place // each


def mask_ranks(normals, rank, vectors):
    rank_cap, sims = normals.shape
    row = lax.broadcasted_iota(jnp.int32, (rank_cap, LANES), 0)
    keep = jnp.where(row < rank, 1.0, 0.0).astype(jnp.bfloat16)
    for tile in range(sims // LANES):
        cols = slice(tile * LANES, (tile + 1) * LANES)
        vectors[:, cols] = normals[:, cols] * keep


def running_sums(rows, vectors, prefix, start):
    count, sims = rows.shape[0], vectors.shape[1]
    for col in range(0, sims, COLS):
        coloured = jnp.dot(rows, vectors[:, col:col + COLS], preferred_element_type=jnp.float32)
        square = coloured * coloured
        for part in range(COLS // LANES):
            tile = col // LANES + part
            lane = slice(part * LANES, (part + 1) * LANES)
            run = prefix[tile, start:start + 8, :]
            for at in range(0, count, 32):
                inner = None
                for row in range(at, at + 32, 8):
                    inner = square[row:row + 8, lane] if inner is None else inner + square[row:row + 8, lane]
                    prefix[tile, start + row + 8:start + row + 16, :] = run + inner
                run = run + inner


def opening_kernel(lens, ranks, factor, normals, prefix, next_factor, next_normals, table,
                   lens_in, ranks_in, factor_in, normals_in, vectors, sems):
    block_count, capacity, _ = factor.shape
    chunks = capacity // CHUNK
    copies = [
        pltpu.make_async_copy(source, target, sems.at[at])
        for at, (source, target) in enumerate(
            [(ranks, ranks_in), (lens, lens_in), (normals.at[0], normals_in)]
            + [(factor.at[0, c * CHUNK:(c + 1) * CHUNK], factor_in.at[c * CHUNK:(c + 1) * CHUNK]) for c in range(chunks)]
            + [(normals.at[k], next_normals.at[k - 1]) for k in range(1, block_count)]
            + [(factor.at[k], next_factor.at[k - 1]) for k in range(1, block_count)]
        )
    ]
    for copy in copies[:3 + chunks]:
        copy.start()
    for tile in range(prefix.shape[0]):
        prefix[tile, 0:8, :] = jnp.zeros((8, LANES), jnp.float32)
    for copy in copies[:3]:
        copy.wait()
    for block in range(block_count):
        table[block:block + 1, :] = jnp.full((1, LANES), ranks_in[block], jnp.int32)
        table[block_count + block:block_count + block + 1, :] = jnp.full((1, LANES), lens_in[block], jnp.int32)
    mask_ranks(normals_in, ranks_in[0], vectors)
    for copy in copies[3 + chunks:]:
        copy.start()
    for chunk in range(chunks):
        copies[3 + chunk].wait()

        @pl.when(chunk * CHUNK < lens_in[0])
        def _():
            rows = slice(chunk * CHUNK, (chunk + 1) * CHUNK)
            running_sums(factor_in[rows, :], vectors, prefix, chunk * CHUNK)
    for copy in copies[3 + chunks:]:
        copy.wait()


def lending_kernel(block_count, classes, table, spans, prefix, out, table_in, spans_in, parts, sems):
    copies = [
        pltpu.make_async_copy(table, table_in, sems.at[0]),
        pltpu.make_async_copy(spans, spans_in, sems.at[1]),
    ]
    for copy in copies:
        copy.start()
    for copy in copies:
        copy.wait()
    genes = spans.shape[1]
    capacity = prefix.shape[1] // block_count - 8
    base = lax.axis_index("genome") * block_count * capacity
    length = table_in[block_count, 0]
    for first in range(0, genes, 8):
        side = first // 8 % parts.shape[0]
        for slot in range(8):
            gene = class_major(first + slot, genes // classes, classes)
            upper = jnp.clip(spans_in[1, gene] - base, 0, length)
            for tile in range(prefix.shape[0]):
                parts[side, tile, slot * 8:slot * 8 + 8, :] = prefix[tile, pl.ds(upper, 8), :]
        reduce_parts(parts, side, out, first)


def closing_kernel(classes, table, spans, lent, factor, normals, old_prefix, prefix, out,
                   table_in, spans_in, vectors, parts, sems):
    del lent, old_prefix
    block_count, capacity = factor.shape[0] + 1, factor.shape[1]
    copies = [
        pltpu.make_async_copy(table, table_in, sems.at[0]),
        pltpu.make_async_copy(spans, spans_in, sems.at[1]),
    ]
    for copy in copies:
        copy.start()
    stride = capacity + 8
    for block in range(1, block_count):
        mask_ranks(normals.at[block - 1], table[block:block + 1, :], vectors)
        if block == 1:
            for copy in copies:
                copy.wait()
            length = [table_in[block_count + k, 0] for k in range(block_count)]
        for tile in range(prefix.shape[0]):
            carry = prefix[tile, pl.ds((block - 1) * stride + length[block - 1], 8), :]
            prefix[tile, block * stride:block * stride + 8, :] = carry
        for chunk in range(capacity // CHUNK):
            @pl.when(chunk * CHUNK < length[block])
            def _():
                rows = slice(chunk * CHUNK, (chunk + 1) * CHUNK)
                running_sums(factor[block - 1, rows, :], vectors, prefix, block * stride + chunk * CHUNK)

    genes = spans.shape[1]
    base = lax.axis_index("genome") * block_count * capacity

    def place(slot):
        slot = slot - base
        at = jnp.minimum(slot, length[0])
        for block in range(1, block_count):
            here = jnp.minimum(slot - block * capacity, length[block]) + block * stride
            at = jnp.where(slot >= block * capacity, here, at)
        return at

    for first in range(0, genes, 8):
        side = first // 8 % parts.shape[0]
        for slot in range(8):
            gene = class_major(first + slot, genes // classes, classes)
            lower, upper = place(spans_in[0, gene]), place(spans_in[1, gene])
            for tile in range(prefix.shape[0]):
                parts[side, tile, slot * 8:slot * 8 + 8, :] = (
                    prefix[tile, pl.ds(upper, 8), :] - prefix[tile, pl.ds(lower, 8), :]
                )
        reduce_parts(parts, side, out, first)


ANY, IN_VMEM = pl.BlockSpec(memory_space=pl.ANY), pl.BlockSpec(memory_space=VMEM)
IN_HBM = pl.BlockSpec(memory_space=pltpu.MemorySpace.HBM)


def opening(lens, ranks, factor, normals):
    block_count, capacity, rank_cap = factor.shape
    sims = normals.shape[2]
    shape = jax.ShapeDtypeStruct
    return pl.pallas_call(
        opening_kernel,
        out_shape=[
            shape((sims // LANES, block_count * (capacity + 8), LANES), jnp.float32),
            shape((block_count - 1, capacity, rank_cap), factor.dtype),
            shape((block_count - 1, rank_cap, sims), normals.dtype),
            shape((8, LANES), jnp.int32),
        ],
        in_specs=[IN_HBM] * 4,
        out_specs=[IN_VMEM] * 4,
        scratch_shapes=[
            pltpu.SMEM((block_count,), jnp.int32),
            pltpu.SMEM((block_count,), jnp.int32),
            pltpu.VMEM((capacity, rank_cap), factor.dtype),
            pltpu.VMEM((rank_cap, sims), normals.dtype),
            pltpu.VMEM((rank_cap, sims), jnp.bfloat16),
            pltpu.SemaphoreType.DMA((1 + 2 * block_count + capacity // CHUNK,)),
        ],
        compiler_params=pltpu.CompilerParams(vmem_limit_bytes=8 << 20),
        name="opening",
    )(lens, ranks, factor, normals)


def lending(block_count, classes, table, spans, prefix):
    genes = spans.shape[1]
    tiles = prefix.shape[0]
    return pl.pallas_call(
        functools.partial(lending_kernel, block_count, classes),
        out_shape=jax.ShapeDtypeStruct((genes, tiles * LANES), jnp.float32),
        in_specs=[ANY, ANY, IN_VMEM],
        out_specs=IN_VMEM,
        scratch_shapes=[
            pltpu.SMEM((8, LANES), jnp.int32),
            pltpu.SMEM((2, genes), jnp.int32),
            pltpu.VMEM((2, tiles, 64, LANES), jnp.float32),
            pltpu.SemaphoreType.DMA((2,)),
        ],
        compiler_params=pltpu.CompilerParams(vmem_limit_bytes=4 << 20),
        name="lending",
    )(table, spans, prefix)


def closing(classes, table, spans, lent, factor, normals, prefix):
    genes = spans.shape[1]
    tiles = prefix.shape[0]
    _, capacity, rank_cap = factor.shape
    sims = tiles * LANES
    return pl.pallas_call(
        functools.partial(closing_kernel, classes),
        out_shape=[
            jax.ShapeDtypeStruct(prefix.shape, jnp.float32),
            jax.ShapeDtypeStruct((genes, sims), jnp.float32),
        ],
        in_specs=[IN_VMEM, ANY, ANY] + [IN_VMEM] * 3,
        out_specs=[IN_VMEM] * 2,
        input_output_aliases={5: 0},
        scratch_shapes=[
            pltpu.SMEM((8, LANES), jnp.int32),
            pltpu.SMEM((2, genes), jnp.int32),
            pltpu.VMEM((rank_cap, sims), jnp.bfloat16),
            pltpu.VMEM((2, tiles, 64, LANES), jnp.float32),
            pltpu.SemaphoreType.DMA((2,)),
        ],
        compiler_params=pltpu.CompilerParams(vmem_limit_bytes=8 << 20),
        cost_estimate=pl.CostEstimate(
            flops=6 * capacity * rank_cap * sims, bytes_accessed=16 << 20, transcendentals=0
        ),
        name="closing",
    )(table, spans, lent, factor, normals, prefix)


def combine_kernel(classes, capacity, held, back, *refs):
    outs, stat = refs[:-1], refs[-1]
    each = outs[0].shape[0]
    total = (held[...] + back[...]) / capacity
    for at in range(classes):
        stat[at] = total[at * each:(at + 1) * each]
    plane = lax.axis_index("genome") // QUAD
    for apart in range(classes):
        outs[apart][...] = stat[plane ^ apart].astype(jnp.bfloat16)


def combine(classes, capacity, parts):
    genes, sims = parts[0].shape
    piece = jax.ShapeDtypeStruct((genes // classes, sims), jnp.bfloat16)
    return pl.pallas_call(
        functools.partial(combine_kernel, classes, capacity),
        out_shape=[piece] * classes,
        in_specs=[pl.BlockSpec(memory_space=VMEM)] * 2,
        out_specs=[pl.BlockSpec(memory_space=VMEM)] * classes,
        scratch_shapes=[pltpu.VMEM((classes, genes // classes, sims), jnp.float32)],
        compiler_params=pltpu.CompilerParams(vmem_limit_bytes=8 << 20),
        name="combine",
    )(*parts)


def member_kernel(classes, flips, genes_dev, paths, member, share):
    device = lax.axis_index("genome")
    plane, inner = device // QUAD, device % QUAD
    rows, pairs = member.shape
    genes = paths.shape[1]
    each = genes_dev // classes
    own = paths[pl.ds(inner, 1), :] - device * rows
    own = jnp.where((own >= 0) & (own < rows), own, 0).astype(jnp.float32)
    own = jnp.broadcast_to(own, (8, genes)).astype(jnp.bfloat16)
    col = lax.broadcasted_iota(jnp.int32, (genes, pairs), 1)
    gene = lax.broadcasted_iota(jnp.int32, (genes, pairs), 0)
    part = col // genes_dev
    source_in = jnp.zeros(col.shape, jnp.int32)
    for at, flip in enumerate(flips):
        source_in = jnp.where(part == at, inner ^ flip, source_in)
    source_plane = plane ^ ((col % genes_dev) // each)
    source = source_plane * QUAD + source_in
    named = source * genes_dev + (col % each) * classes + plane
    pick = jnp.where(gene == named, 1.0, 0.0).astype(jnp.bfloat16)
    ids = jnp.dot(own, pick, preferred_element_type=jnp.float32)[0:1]
    row = lax.broadcasted_iota(jnp.int32, (rows, pairs), 0).astype(jnp.float32)
    found = jnp.where(row == ids, 1.0, 0.0)
    member[...] = found.astype(jnp.bfloat16)
    share[...] = 1.0 / jnp.sum(found, axis=1, keepdims=True)


def members(classes, flips, genes_dev, rows, paths):
    pairs = QUAD * genes_dev
    return pl.pallas_call(
        functools.partial(member_kernel, classes, flips, genes_dev),
        out_shape=[
            jax.ShapeDtypeStruct((rows, pairs), jnp.bfloat16),
            jax.ShapeDtypeStruct((rows, 1), jnp.float32),
        ],
        in_specs=[pl.BlockSpec(memory_space=VMEM)],
        out_specs=[pl.BlockSpec(memory_space=VMEM)] * 2,
        compiler_params=pltpu.CompilerParams(vmem_limit_bytes=16 << 20),
        name="members",
    )(paths)


def score_kernel(member, share, *refs):
    parts, (out, made, sems) = refs[:-3], refs[-3:]
    copies = []
    for at in range(made.shape[0]):
        cols = slice(at * COLS, (at + 1) * COLS)
        genes = jnp.concatenate([part[:, cols] for part in parts], axis=0)
        made[at] = jnp.dot(member[...], genes, preferred_element_type=jnp.float32) * share[...]
        copies.append(pltpu.make_async_copy(made.at[at], out.at[:, cols], sems.at[at]))
        copies[-1].start()
    for copy in copies:
        copy.wait()


def score(member, share, parts):
    rows, pairs = member.shape
    _, sims = parts[0].shape
    return pl.pallas_call(
        score_kernel,
        out_shape=jax.ShapeDtypeStruct((rows, sims), jnp.float32),
        in_specs=[IN_VMEM] * (2 + len(parts)),
        out_specs=ANY,
        scratch_shapes=[
            pltpu.VMEM((sims // COLS, rows, COLS), jnp.float32),
            pltpu.SemaphoreType.DMA((sims // COLS,)),
        ],
        compiler_params=pltpu.CompilerParams(vmem_limit_bytes=16 << 20),
        name="score",
    )(member, share, *parts)


def local(factor, normals, block_len, block_rank, gene_span, gene_pathways):
    block_count, capacity, _ = factor.shape
    genes = gene_span.shape[0]
    size = lax.axis_size("genome")
    classes = size // QUAD
    send = functools.partial(lax.ppermute, axis_name="genome")

    own = gene_span.T
    before = send(own, perm=[(i, i + 1) for i in range(size - 1)])
    held = lambda x: pltpu.with_memory_space_constraint(x, pltpu.MemorySpace.HBM)
    prefix, next_factor, next_normals, table = opening(*map(held, (block_len, block_rank, factor, normals)))
    lent = lending(block_count, classes, table, before, prefix)
    back = send(lent, perm=[(i + 1, i) for i in range(size - 1)])
    _, sums = closing(classes, table, own, lent, next_factor, next_normals, prefix)
    paths, sums = lax.optimization_barrier((gene_pathways.T, sums))
    rows = PATHWAYS // size
    member, share = members(classes, (0, 2, 1, 3), genes, rows, paths)
    back, member, share = lax.optimization_barrier((back, member, share))
    pieces = combine(classes, float(capacity), [sums, back])

    flip = lambda x, bits: send(x, perm=[(i, i ^ bits) for i in range(size)])
    arrived = [flip(pieces[apart], apart * QUAD) for apart in reversed(range(1, classes))]
    arrived = [pieces[0]] + arrived[::-1]
    mine = jnp.concatenate(arrived, axis=0)
    across = flip(mine, 2)
    partner = flip(mine, 1)
    corner = flip(across, 1)

    return score(member, share, [mine, across, partner, corner])


def solution(mesh):
    in_specs = (
        P(("groups", "genome"), None, None),
        P(("groups", "genome"), None, None),
        P(("groups", "genome")),
        P(("groups", "genome")),
        P(("groups", "genome"), None),
        P("groups", None),
    )
    out_specs = P(("groups", "genome"), None)
    return jax.shard_map(local, mesh=mesh, in_specs=in_specs, out_specs=out_specs, check_vma=False)
```

```python
import functools

import jax
import jax.numpy as jnp
from jax import lax
from jax.experimental import pallas as pl
from jax.experimental.pallas import tpu as pltpu
from jax.sharding import PartitionSpec as P


PATHWAYS = 4096
QUAD = 4
CHUNK = 1024
COLS = 256
LANES = 128
VMEM = pltpu.MemorySpace.VMEM


def reduce_parts(parts, side, out, first):
    for tile in range(parts.shape[1]):
        total = parts[side, tile, pl.ds(0, 8, stride=8), :]
        for sub in range(1, 8):
            total = total + parts[side, tile, pl.ds(sub, 8, stride=8), :]
        out[first:first + 8, tile * LANES:(tile + 1) * LANES] = total


def class_major(place, each, classes):
    return place % each * classes + place // each


def mask_ranks(normals, rank, vectors):
    rank_cap, sims = normals.shape
    row = lax.broadcasted_iota(jnp.int32, (rank_cap, LANES), 0)
    keep = jnp.where(row < rank, 1.0, 0.0).astype(jnp.bfloat16)
    for tile in range(sims // LANES):
        cols = slice(tile * LANES, (tile + 1) * LANES)
        vectors[:, cols] = normals[:, cols] * keep


def running_sums(rows, vectors, prefix, start):
    count, sims = rows.shape[0], vectors.shape[1]
    for col in range(0, sims, COLS):
        coloured = jnp.dot(rows, vectors[:, col:col + COLS], preferred_element_type=jnp.float32)
        square = coloured * coloured
        for part in range(COLS // LANES):
            tile = col // LANES + part
            lane = slice(part * LANES, (part + 1) * LANES)
            run = prefix[tile, start:start + 8, :]
            for at in range(0, count, 32):
                inner = None
                for row in range(at, at + 32, 8):
                    inner = square[row:row + 8, lane] if inner is None else inner + square[row:row + 8, lane]
                    prefix[tile, start + row + 8:start + row + 16, :] = run + inner
                run = run + inner


def opening_kernel(lens, ranks, factor, normals, prefix, next_factor, next_normals, table,
                   lens_in, ranks_in, factor_in, normals_in, vectors, sems):
    block_count, capacity, _ = factor.shape
    chunks = capacity // CHUNK
    copies = [
        pltpu.make_async_copy(source, target, sems.at[at])
        for at, (source, target) in enumerate(
            [(ranks, ranks_in), (lens, lens_in), (normals.at[0], normals_in)]
            + [(factor.at[0, c * CHUNK:(c + 1) * CHUNK], factor_in.at[c * CHUNK:(c + 1) * CHUNK]) for c in range(chunks)]
            + [(normals.at[k], next_normals.at[k - 1]) for k in range(1, block_count)]
            + [(factor.at[k], next_factor.at[k - 1]) for k in range(1, block_count)]
        )
    ]
    for copy in copies[:3 + chunks]:
        copy.start()
    for tile in range(prefix.shape[0]):
        prefix[tile, 0:8, :] = jnp.zeros((8, LANES), jnp.float32)
    for copy in copies[:3]:
        copy.wait()
    for block in range(block_count):
        table[block:block + 1, :] = jnp.full((1, LANES), ranks_in[block], jnp.int32)
        table[block_count + block:block_count + block + 1, :] = jnp.full((1, LANES), lens_in[block], jnp.int32)
    mask_ranks(normals_in, ranks_in[0], vectors)
    for copy in copies[3 + chunks:]:
        copy.start()
    for chunk in range(chunks):
        copies[3 + chunk].wait()

        @pl.when(chunk * CHUNK < lens_in[0])
        def _():
            rows = slice(chunk * CHUNK, (chunk + 1) * CHUNK)
            running_sums(factor_in[rows, :], vectors, prefix, chunk * CHUNK)
    for copy in copies[3 + chunks:]:
        copy.wait()


def lending_kernel(block_count, classes, table, spans, prefix, out, table_in, spans_in, parts, sems):
    copies = [
        pltpu.make_async_copy(table, table_in, sems.at[0]),
        pltpu.make_async_copy(spans, spans_in, sems.at[1]),
    ]
    for copy in copies:
        copy.start()
    for copy in copies:
        copy.wait()
    genes = spans.shape[1]
    capacity = prefix.shape[1] // block_count - 8
    base = lax.axis_index("genome") * block_count * capacity
    length = table_in[block_count, 0]
    for first in range(0, genes, 8):
        side = first // 8 % parts.shape[0]
        ends = []
        for slot in range(8):
            gene = class_major(first + slot, genes // classes, classes)
            ends.append(jnp.clip(spans_in[1, gene] - base, 0, length))
        reach = functools.reduce(jnp.maximum, ends)

        @pl.when(reach > 0)
        def _():
            for slot, end in enumerate(ends):
                for tile in range(prefix.shape[0]):
                    parts[side, tile, slot * 8:slot * 8 + 8, :] = prefix[tile, pl.ds(end, 8), :]
            reduce_parts(parts, side, out, first)

        @pl.when(reach == 0)
        def _():
            out[first:first + 8, :] = jnp.zeros((8, out.shape[1]), jnp.float32)


def closing_kernel(classes, table, spans, lent, factor, normals, old_prefix, prefix, out,
                   table_in, spans_in, vectors, parts, sems):
    del lent, old_prefix
    block_count, capacity = factor.shape[0] + 1, factor.shape[1]
    copies = [
        pltpu.make_async_copy(table, table_in, sems.at[0]),
        pltpu.make_async_copy(spans, spans_in, sems.at[1]),
    ]
    for copy in copies:
        copy.start()
    stride = capacity + 8
    for block in range(1, block_count):
        mask_ranks(normals.at[block - 1], table[block:block + 1, :], vectors)
        if block == 1:
            for copy in copies:
                copy.wait()
            length = [table_in[block_count + k, 0] for k in range(block_count)]
        for tile in range(prefix.shape[0]):
            carry = prefix[tile, pl.ds((block - 1) * stride + length[block - 1], 8), :]
            prefix[tile, block * stride:block * stride + 8, :] = carry
        for chunk in range(capacity // CHUNK):
            @pl.when(chunk * CHUNK < length[block])
            def _():
                rows = slice(chunk * CHUNK, (chunk + 1) * CHUNK)
                running_sums(factor[block - 1, rows, :], vectors, prefix, block * stride + chunk * CHUNK)

    genes = spans.shape[1]
    base = lax.axis_index("genome") * block_count * capacity

    def place(slot):
        slot = slot - base
        at = jnp.minimum(slot, length[0])
        for block in range(1, block_count):
            here = jnp.minimum(slot - block * capacity, length[block]) + block * stride
            at = jnp.where(slot >= block * capacity, here, at)
        return at

    for first in range(0, genes, 8):
        side = first // 8 % parts.shape[0]
        for slot in range(8):
            gene = class_major(first + slot, genes // classes, classes)
            lower, upper = place(spans_in[0, gene]), place(spans_in[1, gene])
            for tile in range(prefix.shape[0]):
                parts[side, tile, slot * 8:slot * 8 + 8, :] = (
                    prefix[tile, pl.ds(upper, 8), :] - prefix[tile, pl.ds(lower, 8), :]
                )
        reduce_parts(parts, side, out, first)


ANY, IN_VMEM = pl.BlockSpec(memory_space=pl.ANY), pl.BlockSpec(memory_space=VMEM)
IN_HBM = pl.BlockSpec(memory_space=pltpu.MemorySpace.HBM)


def opening(lens, ranks, factor, normals):
    block_count, capacity, rank_cap = factor.shape
    sims = normals.shape[2]
    shape = jax.ShapeDtypeStruct
    return pl.pallas_call(
        opening_kernel,
        out_shape=[
            shape((sims // LANES, block_count * (capacity + 8), LANES), jnp.float32),
            shape((block_count - 1, capacity, rank_cap), factor.dtype),
            shape((block_count - 1, rank_cap, sims), normals.dtype),
            shape((8, LANES), jnp.int32),
        ],
        in_specs=[IN_HBM] * 4,
        out_specs=[IN_VMEM] * 4,
        scratch_shapes=[
            pltpu.SMEM((block_count,), jnp.int32),
            pltpu.SMEM((block_count,), jnp.int32),
            pltpu.VMEM((capacity, rank_cap), factor.dtype),
            pltpu.VMEM((rank_cap, sims), normals.dtype),
            pltpu.VMEM((rank_cap, sims), jnp.bfloat16),
            pltpu.SemaphoreType.DMA((1 + 2 * block_count + capacity // CHUNK,)),
        ],
        compiler_params=pltpu.CompilerParams(vmem_limit_bytes=8 << 20),
        name="opening",
    )(lens, ranks, factor, normals)


def lending(block_count, classes, table, spans, prefix):
    genes = spans.shape[1]
    tiles = prefix.shape[0]
    return pl.pallas_call(
        functools.partial(lending_kernel, block_count, classes),
        out_shape=jax.ShapeDtypeStruct((genes, tiles * LANES), jnp.float32),
        in_specs=[ANY, ANY, IN_VMEM],
        out_specs=IN_VMEM,
        scratch_shapes=[
            pltpu.SMEM((8, LANES), jnp.int32),
            pltpu.SMEM((2, genes), jnp.int32),
            pltpu.VMEM((2, tiles, 64, LANES), jnp.float32),
            pltpu.SemaphoreType.DMA((2,)),
        ],
        compiler_params=pltpu.CompilerParams(vmem_limit_bytes=4 << 20),
        name="lending",
    )(table, spans, prefix)


def closing(classes, table, spans, lent, factor, normals, prefix):
    genes = spans.shape[1]
    tiles = prefix.shape[0]
    _, capacity, rank_cap = factor.shape
    sims = tiles * LANES
    return pl.pallas_call(
        functools.partial(closing_kernel, classes),
        out_shape=[
            jax.ShapeDtypeStruct(prefix.shape, jnp.float32),
            jax.ShapeDtypeStruct((genes, sims), jnp.float32),
        ],
        in_specs=[IN_VMEM, ANY, ANY] + [IN_VMEM] * 3,
        out_specs=[IN_VMEM] * 2,
        input_output_aliases={5: 0},
        scratch_shapes=[
            pltpu.SMEM((8, LANES), jnp.int32),
            pltpu.SMEM((2, genes), jnp.int32),
            pltpu.VMEM((rank_cap, sims), jnp.bfloat16),
            pltpu.VMEM((2, tiles, 64, LANES), jnp.float32),
            pltpu.SemaphoreType.DMA((2,)),
        ],
        compiler_params=pltpu.CompilerParams(vmem_limit_bytes=8 << 20),
        cost_estimate=pl.CostEstimate(
            flops=6 * capacity * rank_cap * sims, bytes_accessed=16 << 20, transcendentals=0
        ),
        name="closing",
    )(table, spans, lent, factor, normals, prefix)


def combine_kernel(classes, capacity, held, back, *refs):
    outs, stat = refs[:-1], refs[-1]
    each = outs[0].shape[0]
    total = (held[...] + back[...]) / capacity
    for at in range(classes):
        stat[at] = total[at * each:(at + 1) * each]
    plane = lax.axis_index("genome") // QUAD
    for apart in range(classes):
        outs[apart][...] = stat[plane ^ apart].astype(jnp.bfloat16)


def combine(classes, capacity, parts):
    genes, sims = parts[0].shape
    piece = jax.ShapeDtypeStruct((genes // classes, sims), jnp.bfloat16)
    return pl.pallas_call(
        functools.partial(combine_kernel, classes, capacity),
        out_shape=[piece] * classes,
        in_specs=[pl.BlockSpec(memory_space=VMEM)] * 2,
        out_specs=[pl.BlockSpec(memory_space=VMEM)] * classes,
        scratch_shapes=[pltpu.VMEM((classes, genes // classes, sims), jnp.float32)],
        compiler_params=pltpu.CompilerParams(vmem_limit_bytes=8 << 20),
        name="combine",
    )(*parts)


def member_kernel(classes, flips, genes_dev, paths, member, share):
    device = lax.axis_index("genome")
    plane, inner = device // QUAD, device % QUAD
    rows, pairs = member.shape
    genes = paths.shape[1]
    each = genes_dev // classes
    own = paths[pl.ds(inner, 1), :] - device * rows
    own = jnp.where((own >= 0) & (own < rows), own, 0).astype(jnp.float32)
    own = jnp.broadcast_to(own, (8, genes)).astype(jnp.bfloat16)
    col = lax.broadcasted_iota(jnp.int32, (genes, pairs), 1)
    gene = lax.broadcasted_iota(jnp.int32, (genes, pairs), 0)
    part = col // genes_dev
    source_in = jnp.zeros(col.shape, jnp.int32)
    for at, flip in enumerate(flips):
        source_in = jnp.where(part == at, inner ^ flip, source_in)
    step = (col % genes_dev) // each
    source_plane = plane ^ jnp.where(step == 0, 0, classes - step)
    source = source_plane * QUAD + source_in
    named = source * genes_dev + (col % each) * classes + plane
    pick = jnp.where(gene == named, 1.0, 0.0).astype(jnp.bfloat16)
    ids = jnp.dot(own, pick, preferred_element_type=jnp.float32)[0:1]
    row = lax.broadcasted_iota(jnp.int32, (rows, pairs), 0).astype(jnp.float32)
    found = jnp.where(row == ids, 1.0, 0.0)
    member[...] = found.astype(jnp.bfloat16)
    share[...] = 1.0 / jnp.sum(found, axis=1, keepdims=True)


def members(classes, flips, genes_dev, rows, paths):
    pairs = QUAD * genes_dev
    return pl.pallas_call(
        functools.partial(member_kernel, classes, flips, genes_dev),
        out_shape=[
            jax.ShapeDtypeStruct((rows, pairs), jnp.bfloat16),
            jax.ShapeDtypeStruct((rows, 1), jnp.float32),
        ],
        in_specs=[pl.BlockSpec(memory_space=VMEM)],
        out_specs=[pl.BlockSpec(memory_space=VMEM)] * 2,
        compiler_params=pltpu.CompilerParams(vmem_limit_bytes=16 << 20),
        name="members",
    )(paths)


def score_kernel(member, share, *refs):
    parts, (out, made, sems) = refs[:-3], refs[-3:]
    copies = []
    for at in range(made.shape[0]):
        cols = slice(at * COLS, (at + 1) * COLS)
        genes = jnp.concatenate([part[:, cols] for part in parts], axis=0)
        made[at] = jnp.dot(member[...], genes, preferred_element_type=jnp.float32) * share[...]
        copies.append(pltpu.make_async_copy(made.at[at], out.at[:, cols], sems.at[at]))
        copies[-1].start()
    for copy in copies:
        copy.wait()


def score(member, share, parts):
    rows, _ = member.shape
    _, sims = parts[0].shape
    return pl.pallas_call(
        score_kernel,
        out_shape=jax.ShapeDtypeStruct((rows, sims), jnp.float32),
        in_specs=[IN_VMEM] * (2 + len(parts)),
        out_specs=ANY,
        scratch_shapes=[
            pltpu.VMEM((sims // COLS, rows, COLS), jnp.float32),
            pltpu.SemaphoreType.DMA((sims // COLS,)),
        ],
        compiler_params=pltpu.CompilerParams(vmem_limit_bytes=16 << 20),
        name="score",
    )(member, share, *parts)


def local(factor, normals, block_len, block_rank, gene_span, gene_pathways):
    block_count, capacity, _ = factor.shape
    genes = gene_span.shape[0]
    size = lax.axis_size("genome")
    classes = size // QUAD
    send = functools.partial(lax.ppermute, axis_name="genome")

    own = gene_span.T
    before = send(own, perm=[(i, i + 1) for i in range(size - 1)])
    held = lambda x: pltpu.with_memory_space_constraint(x, pltpu.MemorySpace.HBM)
    prefix, next_factor, next_normals, table = opening(*map(held, (block_len, block_rank, factor, normals)))
    lent = lending(block_count, classes, table, before, prefix)
    back = send(lent, perm=[(i + 1, i) for i in range(size - 1)])
    _, sums = closing(classes, table, own, lent, next_factor, next_normals, prefix)
    pieces = combine(classes, float(capacity), [sums, back])

    def flip(x, bits):
        return send(x, perm=[(i, i ^ bits) for i in range(size)])

    arrived = [pieces[0]]
    for apart in reversed(range(1, classes)):
        arrived.append(flip(pieces[apart], apart * QUAD))
    half = classes // 2
    early, late = jnp.concatenate(arrived[:half], axis=0), jnp.concatenate(arrived[half:], axis=0)
    across_early = flip(early, 2)
    across_late = flip(late, 2)
    partner = flip(jnp.concatenate([early, late], axis=0), 1)
    corner_early = flip(across_early, 1)
    corner_late = flip(across_late, 1)
    member, share = members(classes, (0, 2, 1, 3), genes, PATHWAYS // size, gene_pathways.T)
    return score(member, share, [early, late, across_early, across_late, partner, corner_early, corner_late])


def solution(mesh):
    in_specs = (
        P(("groups", "genome"), None, None),
        P(("groups", "genome"), None, None),
        P(("groups", "genome")),
        P(("groups", "genome")),
        P(("groups", "genome"), None),
        P("groups", None),
    )
    out_specs = P(("groups", "genome"), None)
    return jax.shard_map(local, mesh=mesh, in_specs=in_specs, out_specs=out_specs, check_vma=False)
```

```python
import functools

import jax
import jax.numpy as jnp
from jax import lax
from jax.experimental import pallas as pl
from jax.experimental.pallas import tpu as pltpu
from jax.sharding import PartitionSpec as P


PATHWAYS = 4096
QUAD = 4
CHUNK = 1024
COLS = 256
LANES = 128
VMEM = pltpu.MemorySpace.VMEM


def reduce_parts(parts, side, out, first):
    for tile in range(parts.shape[1]):
        total = parts[side, tile, pl.ds(0, 8, stride=8), :]
        for sub in range(1, 8):
            total = total + parts[side, tile, pl.ds(sub, 8, stride=8), :]
        out[first:first + 8, tile * LANES:(tile + 1) * LANES] = total


def class_major(place, each, classes):
    return place % each * classes + place // each


def mask_ranks(normals, rank, vectors):
    rank_cap, sims = normals.shape
    row = lax.broadcasted_iota(jnp.int32, (rank_cap, LANES), 0)
    keep = jnp.where(row < rank, 1.0, 0.0).astype(jnp.bfloat16)
    for tile in range(sims // LANES):
        cols = slice(tile * LANES, (tile + 1) * LANES)
        vectors[:, cols] = normals[:, cols] * keep


def running_sums(rows, vectors, prefix, start):
    count, sims = rows.shape[0], vectors.shape[1]
    for col in range(0, sims, COLS):
        coloured = jnp.dot(rows, vectors[:, col:col + COLS], preferred_element_type=jnp.float32)
        square = coloured * coloured
        for part in range(COLS // LANES):
            tile = col // LANES + part
            lane = slice(part * LANES, (part + 1) * LANES)
            run = prefix[tile, start:start + 8, :]
            for at in range(0, count, 32):
                inner = None
                for row in range(at, at + 32, 8):
                    inner = square[row:row + 8, lane] if inner is None else inner + square[row:row + 8, lane]
                    prefix[tile, start + row + 8:start + row + 16, :] = run + inner
                run = run + inner


def opening_kernel(lens, ranks, factor, normals, prefix, next_factor, next_normals, table,
                   lens_in, ranks_in, factor_in, normals_in, vectors, sems):
    block_count, capacity, _ = factor.shape
    chunks = capacity // CHUNK
    copies = [
        pltpu.make_async_copy(source, target, sems.at[at])
        for at, (source, target) in enumerate(
            [(ranks, ranks_in), (lens, lens_in), (normals.at[0], normals_in)]
            + [(factor.at[0, c * CHUNK:(c + 1) * CHUNK], factor_in.at[c * CHUNK:(c + 1) * CHUNK]) for c in range(chunks)]
            + [(normals.at[k], next_normals.at[k - 1]) for k in range(1, block_count)]
            + [(factor.at[k], next_factor.at[k - 1]) for k in range(1, block_count)]
        )
    ]
    for copy in copies[:3 + chunks]:
        copy.start()
    for tile in range(prefix.shape[0]):
        prefix[tile, 0:8, :] = jnp.zeros((8, LANES), jnp.float32)
    for copy in copies[:3]:
        copy.wait()
    for block in range(block_count):
        table[block:block + 1, :] = jnp.full((1, LANES), ranks_in[block], jnp.int32)
        table[block_count + block:block_count + block + 1, :] = jnp.full((1, LANES), lens_in[block], jnp.int32)
    mask_ranks(normals_in, ranks_in[0], vectors)
    for copy in copies[3 + chunks:]:
        copy.start()
    for chunk in range(chunks):
        copies[3 + chunk].wait()

        @pl.when(chunk * CHUNK < lens_in[0])
        def _():
            rows = slice(chunk * CHUNK, (chunk + 1) * CHUNK)
            running_sums(factor_in[rows, :], vectors, prefix, chunk * CHUNK)
    for copy in copies[3 + chunks:]:
        copy.wait()


def lending_kernel(block_count, classes, table, spans, prefix, out, table_in, spans_in, parts, sems):
    copies = [
        pltpu.make_async_copy(table, table_in, sems.at[0]),
        pltpu.make_async_copy(spans, spans_in, sems.at[1]),
    ]
    for copy in copies:
        copy.start()
    for copy in copies:
        copy.wait()
    genes = spans.shape[1]
    capacity = prefix.shape[1] // block_count - 8
    device = lax.axis_index("genome")
    base = device * block_count * capacity
    length = jnp.where(device == 0, 0, table_in[block_count, 0])
    for first in range(0, genes, 8):
        side = first // 8 % parts.shape[0]
        ends = []
        for slot in range(8):
            gene = class_major(first + slot, genes // classes, classes)
            ends.append(jnp.clip(spans_in[1, gene] - base, 0, length))
        reach = functools.reduce(jnp.maximum, ends)

        @pl.when(reach > 0)
        def _():
            for slot, end in enumerate(ends):
                for tile in range(prefix.shape[0]):
                    parts[side, tile, slot * 8:slot * 8 + 8, :] = prefix[tile, pl.ds(end, 8), :]
            reduce_parts(parts, side, out, first)

        @pl.when(reach == 0)
        def _():
            out[first:first + 8, :] = jnp.zeros((8, out.shape[1]), jnp.float32)


def closing_kernel(classes, table, spans, lent, factor, normals, old_prefix, prefix, out,
                   table_in, spans_in, vectors, parts, sems):
    del lent, old_prefix
    block_count, capacity = factor.shape[0] + 1, factor.shape[1]
    copies = [
        pltpu.make_async_copy(table, table_in, sems.at[0]),
        pltpu.make_async_copy(spans, spans_in, sems.at[1]),
    ]
    for copy in copies:
        copy.start()
    stride = capacity + 8
    for block in range(1, block_count):
        mask_ranks(normals.at[block - 1], table[block:block + 1, :], vectors)
        if block == 1:
            for copy in copies:
                copy.wait()
            length = [table_in[block_count + k, 0] for k in range(block_count)]
        for tile in range(prefix.shape[0]):
            carry = prefix[tile, pl.ds((block - 1) * stride + length[block - 1], 8), :]
            prefix[tile, block * stride:block * stride + 8, :] = carry
        for chunk in range(capacity // CHUNK):
            @pl.when(chunk * CHUNK < length[block])
            def _():
                rows = slice(chunk * CHUNK, (chunk + 1) * CHUNK)
                running_sums(factor[block - 1, rows, :], vectors, prefix, block * stride + chunk * CHUNK)

    genes = spans.shape[1]
    base = lax.axis_index("genome") * block_count * capacity

    def place(slot):
        slot = slot - base
        at = jnp.minimum(slot, length[0])
        for block in range(1, block_count):
            here = jnp.minimum(slot - block * capacity, length[block]) + block * stride
            at = jnp.where(slot >= block * capacity, here, at)
        return at

    for first in range(0, genes, 8):
        side = first // 8 % parts.shape[0]
        for slot in range(8):
            gene = class_major(first + slot, genes // classes, classes)
            lower, upper = place(spans_in[0, gene]), place(spans_in[1, gene])
            for tile in range(prefix.shape[0]):
                parts[side, tile, slot * 8:slot * 8 + 8, :] = (
                    prefix[tile, pl.ds(upper, 8), :] - prefix[tile, pl.ds(lower, 8), :]
                )
        reduce_parts(parts, side, out, first)


ANY, IN_VMEM = pl.BlockSpec(memory_space=pl.ANY), pl.BlockSpec(memory_space=VMEM)
IN_HBM = pl.BlockSpec(memory_space=pltpu.MemorySpace.HBM)


def opening(lens, ranks, factor, normals):
    block_count, capacity, rank_cap = factor.shape
    sims = normals.shape[2]
    shape = jax.ShapeDtypeStruct
    return pl.pallas_call(
        opening_kernel,
        out_shape=[
            shape((sims // LANES, block_count * (capacity + 8), LANES), jnp.float32),
            shape((block_count - 1, capacity, rank_cap), factor.dtype),
            shape((block_count - 1, rank_cap, sims), normals.dtype),
            shape((8, LANES), jnp.int32),
        ],
        in_specs=[IN_HBM] * 4,
        out_specs=[IN_VMEM] * 4,
        scratch_shapes=[
            pltpu.SMEM((block_count,), jnp.int32),
            pltpu.SMEM((block_count,), jnp.int32),
            pltpu.VMEM((capacity, rank_cap), factor.dtype),
            pltpu.VMEM((rank_cap, sims), normals.dtype),
            pltpu.VMEM((rank_cap, sims), jnp.bfloat16),
            pltpu.SemaphoreType.DMA((1 + 2 * block_count + capacity // CHUNK,)),
        ],
        compiler_params=pltpu.CompilerParams(vmem_limit_bytes=8 << 20),
        name="opening",
    )(lens, ranks, factor, normals)


def lending(block_count, classes, table, spans, prefix):
    genes = spans.shape[1]
    tiles = prefix.shape[0]
    return pl.pallas_call(
        functools.partial(lending_kernel, block_count, classes),
        out_shape=jax.ShapeDtypeStruct((genes, tiles * LANES), jnp.float32),
        in_specs=[ANY, ANY, IN_VMEM],
        out_specs=IN_VMEM,
        scratch_shapes=[
            pltpu.SMEM((8, LANES), jnp.int32),
            pltpu.SMEM((2, genes), jnp.int32),
            pltpu.VMEM((2, tiles, 64, LANES), jnp.float32),
            pltpu.SemaphoreType.DMA((2,)),
        ],
        compiler_params=pltpu.CompilerParams(vmem_limit_bytes=4 << 20),
        name="lending",
    )(table, spans, prefix)


def closing(classes, table, spans, lent, factor, normals, prefix):
    genes = spans.shape[1]
    tiles = prefix.shape[0]
    _, capacity, rank_cap = factor.shape
    sims = tiles * LANES
    return pl.pallas_call(
        functools.partial(closing_kernel, classes),
        out_shape=[
            jax.ShapeDtypeStruct(prefix.shape, jnp.float32),
            jax.ShapeDtypeStruct((genes, sims), jnp.float32),
        ],
        in_specs=[IN_VMEM, ANY, ANY] + [IN_VMEM] * 3,
        out_specs=[IN_VMEM] * 2,
        input_output_aliases={5: 0},
        scratch_shapes=[
            pltpu.SMEM((8, LANES), jnp.int32),
            pltpu.SMEM((2, genes), jnp.int32),
            pltpu.VMEM((rank_cap, sims), jnp.bfloat16),
            pltpu.VMEM((2, tiles, 64, LANES), jnp.float32),
            pltpu.SemaphoreType.DMA((2,)),
        ],
        compiler_params=pltpu.CompilerParams(vmem_limit_bytes=8 << 20),
        cost_estimate=pl.CostEstimate(
            flops=6 * capacity * rank_cap * sims, bytes_accessed=16 << 20, transcendentals=0
        ),
        name="closing",
    )(table, spans, lent, factor, normals, prefix)


def combine_kernel(classes, capacity, held, back, *refs):
    outs, stat = refs[:-1], refs[-1]
    each = outs[0].shape[0]
    total = (held[...] + back[...]) / capacity
    for at in range(classes):
        stat[at] = total[at * each:(at + 1) * each]
    plane = lax.axis_index("genome") // QUAD
    for apart in range(classes):
        outs[apart][...] = stat[plane ^ apart].astype(jnp.bfloat16)


def combine(classes, capacity, parts):
    genes, sims = parts[0].shape
    piece = jax.ShapeDtypeStruct((genes // classes, sims), jnp.bfloat16)
    return pl.pallas_call(
        functools.partial(combine_kernel, classes, capacity),
        out_shape=[piece] * classes,
        in_specs=[pl.BlockSpec(memory_space=VMEM)] * 2,
        out_specs=[pl.BlockSpec(memory_space=VMEM)] * classes,
        scratch_shapes=[pltpu.VMEM((classes, genes // classes, sims), jnp.float32)],
        compiler_params=pltpu.CompilerParams(vmem_limit_bytes=8 << 20),
        name="combine",
    )(*parts)


def member_kernel(classes, flips, genes_dev, paths, member, share):
    device = lax.axis_index("genome")
    plane, inner = device // QUAD, device % QUAD
    rows, pairs = member.shape
    genes = paths.shape[1]
    each = genes_dev // classes
    own = paths[pl.ds(inner, 1), :] - device * rows
    own = jnp.where((own >= 0) & (own < rows), own, 0).astype(jnp.float32)
    own = jnp.broadcast_to(own, (8, genes)).astype(jnp.bfloat16)
    col = lax.broadcasted_iota(jnp.int32, (genes, pairs), 1)
    gene = lax.broadcasted_iota(jnp.int32, (genes, pairs), 0)
    part = col // genes_dev
    source_in = jnp.zeros(col.shape, jnp.int32)
    for at, flip in enumerate(flips):
        source_in = jnp.where(part == at, inner ^ flip, source_in)
    step = (col % genes_dev) // each
    source_plane = plane ^ jnp.where(step == 0, 0, classes - step)
    source = source_plane * QUAD + source_in
    named = source * genes_dev + (col % each) * classes + plane
    pick = jnp.where(gene == named, 1.0, 0.0).astype(jnp.bfloat16)
    ids = jnp.dot(own, pick, preferred_element_type=jnp.float32)[0:1]
    row = lax.broadcasted_iota(jnp.int32, (rows, pairs), 0).astype(jnp.float32)
    found = jnp.where(row == ids, 1.0, 0.0)
    member[...] = found.astype(jnp.bfloat16)
    share[...] = 1.0 / jnp.sum(found, axis=1, keepdims=True)


def members(classes, flips, genes_dev, rows, paths):
    pairs = QUAD * genes_dev
    return pl.pallas_call(
        functools.partial(member_kernel, classes, flips, genes_dev),
        out_shape=[
            jax.ShapeDtypeStruct((rows, pairs), jnp.bfloat16),
            jax.ShapeDtypeStruct((rows, 1), jnp.float32),
        ],
        in_specs=[pl.BlockSpec(memory_space=VMEM)],
        out_specs=[pl.BlockSpec(memory_space=VMEM)] * 2,
        compiler_params=pltpu.CompilerParams(vmem_limit_bytes=16 << 20),
        name="members",
    )(paths)


def score_kernel(member, share, *refs):
    parts, (out, made, sems) = refs[:-3], refs[-3:]
    copies = []
    for at in range(made.shape[0]):
        cols = slice(at * COLS, (at + 1) * COLS)
        genes = jnp.concatenate([part[:, cols] for part in parts], axis=0)
        made[at] = jnp.dot(member[...], genes, preferred_element_type=jnp.float32) * share[...]
        copies.append(pltpu.make_async_copy(made.at[at], out.at[:, cols], sems.at[at]))
        copies[-1].start()
    for copy in copies:
        copy.wait()


def score(member, share, parts):
    rows, _ = member.shape
    _, sims = parts[0].shape
    return pl.pallas_call(
        score_kernel,
        out_shape=jax.ShapeDtypeStruct((rows, sims), jnp.float32),
        in_specs=[IN_VMEM] * (2 + len(parts)),
        out_specs=ANY,
        scratch_shapes=[
            pltpu.VMEM((sims // COLS, rows, COLS), jnp.float32),
            pltpu.SemaphoreType.DMA((sims // COLS,)),
        ],
        compiler_params=pltpu.CompilerParams(vmem_limit_bytes=16 << 20),
        name="score",
    )(member, share, *parts)


def local(factor, normals, block_len, block_rank, gene_span, gene_pathways):
    block_count, capacity, _ = factor.shape
    genes = gene_span.shape[0]
    size = lax.axis_size("genome")
    classes = size // QUAD
    send = functools.partial(lax.ppermute, axis_name="genome")

    own = gene_span.T
    before = send(own, perm=[(i, (i + 1) % size) for i in range(size)])
    held = lambda x: pltpu.with_memory_space_constraint(x, pltpu.MemorySpace.HBM)
    prefix, next_factor, next_normals, table = opening(*map(held, (block_len, block_rank, factor, normals)))
    lent = lending(block_count, classes, table, before, prefix)
    back = send(lent, perm=[((i + 1) % size, i) for i in range(size)])
    _, sums = closing(classes, table, own, lent, next_factor, next_normals, prefix)
    pieces = combine(classes, float(capacity), [sums, back])

    def flip(x, bits):
        return send(x, perm=[(i, i ^ bits) for i in range(size)])

    arrived = [pieces[0]]
    for apart in reversed(range(1, classes)):
        arrived.append(flip(pieces[apart], apart * QUAD))
    half = classes // 2
    early, late = jnp.concatenate(arrived[:half], axis=0), jnp.concatenate(arrived[half:], axis=0)
    across_early = flip(early, 2)
    across_late = flip(late, 2)
    partner = flip(jnp.concatenate([early, late], axis=0), 1)
    corner_early = flip(across_early, 1)
    corner_late = flip(across_late, 1)
    member, share = members(classes, (0, 2, 1, 3), genes, PATHWAYS // size, gene_pathways.T)
    return score(member, share, [early, late, across_early, across_late, partner, corner_early, corner_late])


def solution(mesh):
    in_specs = (
        P(("groups", "genome"), None, None),
        P(("groups", "genome"), None, None),
        P(("groups", "genome")),
        P(("groups", "genome")),
        P(("groups", "genome"), None),
        P("groups", None),
    )
    out_specs = P(("groups", "genome"), None)
    return jax.shard_map(local, mesh=mesh, in_specs=in_specs, out_specs=out_specs, check_vma=False)
```

```python
import functools

import jax
import jax.numpy as jnp
from jax import lax
from jax.experimental import pallas as pl
from jax.experimental.pallas import tpu as pltpu
from jax.sharding import PartitionSpec as P


PATHWAYS = 4096
QUAD = 4
CHUNK = 2048
COLS = 256
LANES = 128
VMEM = pltpu.MemorySpace.VMEM


def order_of(classes):
    return list(range(classes // 2, classes)) + list(range(classes // 2 - 1, 0, -1))


def reduce_parts(parts, side, out, first):
    for tile in range(parts.shape[1]):
        total = parts[side, tile, pl.ds(0, 8, stride=8), :]
        for sub in range(1, 8):
            total = total + parts[side, tile, pl.ds(sub, 8, stride=8), :]
        out[first:first + 8, tile * LANES:(tile + 1) * LANES] = total


def class_major(place, each, classes):
    return place % each * classes + place // each


def mask_ranks(normals, rank, vectors):
    rank_cap, sims = normals.shape
    row = lax.broadcasted_iota(jnp.int32, (rank_cap, LANES), 0)
    keep = jnp.where(row < rank, 1.0, 0.0).astype(jnp.bfloat16)
    for tile in range(sims // LANES):
        cols = slice(tile * LANES, (tile + 1) * LANES)
        vectors[:, cols] = normals[:, cols] * keep


def running_sums(rows, vectors, prefix, start):
    count, sims = rows.shape[0], vectors.shape[1]
    for col in range(0, sims, COLS):
        coloured = jnp.dot(rows, vectors[:, col:col + COLS], preferred_element_type=jnp.float32)
        square = coloured * coloured
        for part in range(COLS // LANES):
            tile = col // LANES + part
            lane = slice(part * LANES, (part + 1) * LANES)
            run = prefix[tile, start:start + 8, :]
            for at in range(0, count, 32):
                inner = None
                for row in range(at, at + 32, 8):
                    inner = square[row:row + 8, lane] if inner is None else inner + square[row:row + 8, lane]
                    prefix[tile, start + row + 8:start + row + 16, :] = run + inner
                run = run + inner


def opening_kernel(lens, ranks, factor, normals, prefix, next_factor, next_normals, table,
                   lens_in, ranks_in, factor_in, normals_in, vectors, sems):
    block_count, capacity, _ = factor.shape
    chunks = capacity // CHUNK
    copies = [
        pltpu.make_async_copy(source, target, sems.at[at])
        for at, (source, target) in enumerate(
            [(ranks, ranks_in), (lens, lens_in), (normals.at[0], normals_in)]
            + [(factor.at[0, c * CHUNK:(c + 1) * CHUNK], factor_in.at[c * CHUNK:(c + 1) * CHUNK]) for c in range(chunks)]
            + [(normals.at[k], next_normals.at[k - 1]) for k in range(1, block_count)]
            + [(factor.at[k], next_factor.at[k - 1]) for k in range(1, block_count)]
        )
    ]
    for copy in copies[:3 + chunks]:
        copy.start()
    for tile in range(prefix.shape[0]):
        prefix[tile, 0:8, :] = jnp.zeros((8, LANES), jnp.float32)
    for copy in copies[:3]:
        copy.wait()
    for block in range(block_count):
        table[block:block + 1, :] = jnp.full((1, LANES), ranks_in[block], jnp.int32)
        table[block_count + block:block_count + block + 1, :] = jnp.full((1, LANES), lens_in[block], jnp.int32)
    mask_ranks(normals_in, ranks_in[0], vectors)
    for copy in copies[3 + chunks:]:
        copy.start()
    for chunk in range(chunks):
        copies[3 + chunk].wait()

        @pl.when(chunk * CHUNK < lens_in[0])
        def _():
            rows = slice(chunk * CHUNK, (chunk + 1) * CHUNK)
            running_sums(factor_in[rows, :], vectors, prefix, chunk * CHUNK)
    for copy in copies[3 + chunks:]:
        copy.wait()


def lending_kernel(block_count, classes, table, spans, prefix, out, table_in, spans_in, parts, sems):
    copies = [
        pltpu.make_async_copy(table, table_in, sems.at[0]),
        pltpu.make_async_copy(spans, spans_in, sems.at[1]),
    ]
    for copy in copies:
        copy.start()
    for copy in copies:
        copy.wait()
    genes = spans.shape[1]
    capacity = prefix.shape[1] // block_count - 8
    device = lax.axis_index("genome")
    base = jnp.where(device == 0, 1 << 30, device * block_count * capacity)
    length = table_in[block_count, 0]
    for first in range(0, genes, 8):
        side = first // 8 % parts.shape[0]
        ends = []
        for slot in range(8):
            gene = class_major(first + slot, genes // classes, classes)
            ends.append(spans_in[1, gene])
        reach = functools.reduce(jnp.maximum, ends)

        @pl.when(reach > base)
        def _():
            for slot, end in enumerate(ends):
                end = jnp.clip(end - base, 0, length)
                for tile in range(prefix.shape[0]):
                    parts[side, tile, slot * 8:slot * 8 + 8, :] = prefix[tile, pl.ds(end, 8), :]
            reduce_parts(parts, side, out, first)

        @pl.when(reach <= base)
        def _():
            out[first:first + 8, :] = jnp.zeros((8, out.shape[1]), jnp.float32)


def closing_kernel(classes, table, spans, lent, factor, normals, old_prefix, prefix, out,
                   table_in, spans_in, vectors, parts, sems):
    del lent, old_prefix
    block_count, capacity = factor.shape[0] + 1, factor.shape[1]
    copies = [
        pltpu.make_async_copy(table, table_in, sems.at[0]),
        pltpu.make_async_copy(spans, spans_in, sems.at[1]),
    ]
    for copy in copies:
        copy.start()
    stride = capacity + 8
    for block in range(1, block_count):
        mask_ranks(normals.at[block - 1], table[block:block + 1, :], vectors)
        if block == 1:
            for copy in copies:
                copy.wait()
            length = [table_in[block_count + k, 0] for k in range(block_count)]
        for tile in range(prefix.shape[0]):
            carry = prefix[tile, pl.ds((block - 1) * stride + length[block - 1], 8), :]
            prefix[tile, block * stride:block * stride + 8, :] = carry
        for chunk in range(capacity // CHUNK):
            @pl.when(chunk * CHUNK < length[block])
            def _():
                rows = slice(chunk * CHUNK, (chunk + 1) * CHUNK)
                running_sums(factor[block - 1, rows, :], vectors, prefix, block * stride + chunk * CHUNK)

    genes = spans.shape[1]
    base = lax.axis_index("genome") * block_count * capacity

    def place(slot):
        slot = slot - base
        at = jnp.minimum(slot, length[0])
        for block in range(1, block_count):
            here = jnp.minimum(slot - block * capacity, length[block]) + block * stride
            at = jnp.where(slot >= block * capacity, here, at)
        return at

    for first in range(0, genes, 8):
        side = first // 8 % parts.shape[0]
        for slot in range(8):
            gene = class_major(first + slot, genes // classes, classes)
            lower, upper = place(spans_in[0, gene]), place(spans_in[1, gene])
            for tile in range(prefix.shape[0]):
                parts[side, tile, slot * 8:slot * 8 + 8, :] = (
                    prefix[tile, pl.ds(upper, 8), :] - prefix[tile, pl.ds(lower, 8), :]
                )
        reduce_parts(parts, side, out, first)


ANY, IN_VMEM = pl.BlockSpec(memory_space=pl.ANY), pl.BlockSpec(memory_space=VMEM)
IN_HBM = pl.BlockSpec(memory_space=pltpu.MemorySpace.HBM)


def opening(lens, ranks, factor, normals):
    block_count, capacity, rank_cap = factor.shape
    sims = normals.shape[2]
    shape = jax.ShapeDtypeStruct
    return pl.pallas_call(
        opening_kernel,
        out_shape=[
            shape((sims // LANES, block_count * (capacity + 8), LANES), jnp.float32),
            shape((block_count - 1, capacity, rank_cap), factor.dtype),
            shape((block_count - 1, rank_cap, sims), normals.dtype),
            shape((8, LANES), jnp.int32),
        ],
        in_specs=[IN_HBM] * 4,
        out_specs=[IN_VMEM] * 4,
        scratch_shapes=[
            pltpu.SMEM((block_count,), jnp.int32),
            pltpu.SMEM((block_count,), jnp.int32),
            pltpu.VMEM((capacity, rank_cap), factor.dtype),
            pltpu.VMEM((rank_cap, sims), normals.dtype),
            pltpu.VMEM((rank_cap, sims), jnp.bfloat16),
            pltpu.SemaphoreType.DMA((1 + 2 * block_count + capacity // CHUNK,)),
        ],
        compiler_params=pltpu.CompilerParams(vmem_limit_bytes=8 << 20),
        name="opening",
    )(lens, ranks, factor, normals)


def lending(block_count, classes, table, spans, prefix):
    genes = spans.shape[1]
    tiles = prefix.shape[0]
    return pl.pallas_call(
        functools.partial(lending_kernel, block_count, classes),
        out_shape=jax.ShapeDtypeStruct((genes, tiles * LANES), jnp.float32),
        in_specs=[ANY, ANY, IN_VMEM],
        out_specs=IN_VMEM,
        scratch_shapes=[
            pltpu.SMEM((8, LANES), jnp.int32),
            pltpu.SMEM((2, genes), jnp.int32),
            pltpu.VMEM((2, tiles, 64, LANES), jnp.float32),
            pltpu.SemaphoreType.DMA((2,)),
        ],
        compiler_params=pltpu.CompilerParams(vmem_limit_bytes=4 << 20),
        name="lending",
    )(table, spans, prefix)


def closing(classes, table, spans, lent, factor, normals, prefix):
    genes = spans.shape[1]
    tiles = prefix.shape[0]
    _, capacity, rank_cap = factor.shape
    sims = tiles * LANES
    return pl.pallas_call(
        functools.partial(closing_kernel, classes),
        out_shape=[
            jax.ShapeDtypeStruct(prefix.shape, jnp.float32),
            jax.ShapeDtypeStruct((genes, sims), jnp.float32),
        ],
        in_specs=[IN_VMEM, ANY, ANY] + [IN_VMEM] * 3,
        out_specs=[IN_VMEM] * 2,
        input_output_aliases={5: 0},
        scratch_shapes=[
            pltpu.SMEM((8, LANES), jnp.int32),
            pltpu.SMEM((2, genes), jnp.int32),
            pltpu.VMEM((rank_cap, sims), jnp.bfloat16),
            pltpu.VMEM((2, tiles, 64, LANES), jnp.float32),
            pltpu.SemaphoreType.DMA((2,)),
        ],
        compiler_params=pltpu.CompilerParams(vmem_limit_bytes=8 << 20),
        cost_estimate=pl.CostEstimate(
            flops=6 * capacity * rank_cap * sims, bytes_accessed=16 << 20, transcendentals=0
        ),
        name="closing",
    )(table, spans, lent, factor, normals, prefix)


def combine_kernel(classes, capacity, held, back, *refs):
    outs, stat = refs[:-1], refs[-1]
    each = outs[0].shape[0]
    total = (held[...] + back[...]) / capacity
    for at in range(classes):
        stat[at] = total[at * each:(at + 1) * each]
    plane = lax.axis_index("genome") // QUAD
    for apart in range(classes):
        outs[apart][...] = stat[plane ^ apart].astype(jnp.bfloat16)


def combine(classes, capacity, parts):
    genes, sims = parts[0].shape
    piece = jax.ShapeDtypeStruct((genes // classes, sims), jnp.bfloat16)
    return pl.pallas_call(
        functools.partial(combine_kernel, classes, capacity),
        out_shape=[piece] * classes,
        in_specs=[pl.BlockSpec(memory_space=VMEM)] * 2,
        out_specs=[pl.BlockSpec(memory_space=VMEM)] * classes,
        scratch_shapes=[pltpu.VMEM((classes, genes // classes, sims), jnp.float32)],
        compiler_params=pltpu.CompilerParams(vmem_limit_bytes=8 << 20),
        name="combine",
    )(*parts)


def member_kernel(classes, flips, genes_dev, paths, member, share):
    device = lax.axis_index("genome")
    plane, inner = device // QUAD, device % QUAD
    rows, pairs = member.shape
    genes = paths.shape[1]
    each = genes_dev // classes
    own = paths[pl.ds(inner, 1), :] - device * rows
    own = jnp.where((own >= 0) & (own < rows), own, 0).astype(jnp.float32)
    own = jnp.broadcast_to(own, (8, genes)).astype(jnp.bfloat16)
    col = lax.broadcasted_iota(jnp.int32, (genes, pairs), 1)
    gene = lax.broadcasted_iota(jnp.int32, (genes, pairs), 0)
    part = col // genes_dev
    source_in = jnp.zeros(col.shape, jnp.int32)
    for at, flip in enumerate(flips):
        source_in = jnp.where(part == at, inner ^ flip, source_in)
    step = (col % genes_dev) // each
    apart = jnp.zeros(col.shape, jnp.int32)
    for at, planes in enumerate(order_of(classes)):
        apart = jnp.where(step == at + 1, planes, apart)
    source_plane = plane ^ apart
    source = source_plane * QUAD + source_in
    named = source * genes_dev + (col % each) * classes + plane
    pick = jnp.where(gene == named, 1.0, 0.0).astype(jnp.bfloat16)
    ids = jnp.dot(own, pick, preferred_element_type=jnp.float32)[0:1]
    row = lax.broadcasted_iota(jnp.int32, (rows, pairs), 0).astype(jnp.float32)
    found = jnp.where(row == ids, 1.0, 0.0)
    member[...] = found.astype(jnp.bfloat16)
    share[...] = 1.0 / jnp.sum(found, axis=1, keepdims=True)


def members(classes, flips, genes_dev, rows, paths):
    pairs = QUAD * genes_dev
    return pl.pallas_call(
        functools.partial(member_kernel, classes, flips, genes_dev),
        out_shape=[
            jax.ShapeDtypeStruct((rows, pairs), jnp.bfloat16),
            jax.ShapeDtypeStruct((rows, 1), jnp.float32),
        ],
        in_specs=[pl.BlockSpec(memory_space=VMEM)],
        out_specs=[pl.BlockSpec(memory_space=VMEM)] * 2,
        compiler_params=pltpu.CompilerParams(vmem_limit_bytes=16 << 20),
        name="members",
    )(paths)


def score_kernel(member, share, *refs):
    parts, (out, made, sems) = refs[:-3], refs[-3:]
    copies = []
    for at in range(made.shape[0]):
        cols = slice(at * COLS, (at + 1) * COLS)
        genes = jnp.concatenate([part[:, cols] for part in parts], axis=0)
        made[at] = jnp.dot(member[...], genes, preferred_element_type=jnp.float32) * share[...]
        copies.append(pltpu.make_async_copy(made.at[at], out.at[:, cols], sems.at[at]))
        copies[-1].start()
    for copy in copies:
        copy.wait()


def score(member, share, parts):
    rows, _ = member.shape
    _, sims = parts[0].shape
    return pl.pallas_call(
        score_kernel,
        out_shape=jax.ShapeDtypeStruct((rows, sims), jnp.float32),
        in_specs=[IN_VMEM] * (2 + len(parts)),
        out_specs=ANY,
        scratch_shapes=[
            pltpu.VMEM((sims // COLS, rows, COLS), jnp.float32),
            pltpu.SemaphoreType.DMA((sims // COLS,)),
        ],
        compiler_params=pltpu.CompilerParams(vmem_limit_bytes=16 << 20),
        name="score",
    )(member, share, *parts)


def local(factor, normals, block_len, block_rank, gene_span, gene_pathways):
    block_count, capacity, _ = factor.shape
    genes = gene_span.shape[0]
    size = lax.axis_size("genome")
    classes = size // QUAD
    send = functools.partial(lax.ppermute, axis_name="genome")

    own = gene_span.T
    before = send(own, perm=[(i, (i + 1) % size) for i in range(size)])
    held = lambda x: pltpu.with_memory_space_constraint(x, pltpu.MemorySpace.HBM)
    prefix, next_factor, next_normals, table = opening(*map(held, (block_len, block_rank, factor, normals)))
    lent = lending(block_count, classes, table, before, prefix)
    back = send(lent, perm=[((i + 1) % size, i) for i in range(size)])
    _, sums = closing(classes, table, own, lent, next_factor, next_normals, prefix)
    pieces = combine(classes, float(capacity), [sums, back])

    def flip(x, bits):
        return send(x, perm=[(i, i ^ bits) for i in range(size)])

    arrived = [pieces[0]]
    for apart in order_of(classes):
        arrived.append(flip(pieces[apart], apart * QUAD))
    half = classes // 2
    early, late = jnp.concatenate(arrived[:half], axis=0), jnp.concatenate(arrived[half:], axis=0)
    across_early = flip(early, 2)
    across_late = flip(late, 2)
    partner = flip(jnp.concatenate([early, late], axis=0), 1)
    corner_early = flip(across_early, 1)
    corner_late = flip(across_late, 1)
    member, share = members(classes, (0, 2, 1, 3), genes, PATHWAYS // size, gene_pathways.T)
    return score(member, share, [early, late, across_early, across_late, partner, corner_early, corner_late])


def solution(mesh):
    in_specs = (
        P(("groups", "genome"), None, None),
        P(("groups", "genome"), None, None),
        P(("groups", "genome")),
        P(("groups", "genome")),
        P(("groups", "genome"), None),
        P("groups", None),
    )
    out_specs = P(("groups", "genome"), None)
    return jax.shard_map(local, mesh=mesh, in_specs=in_specs, out_specs=out_specs, check_vma=False)
```
